256 devices in a mesh: sector: 128 (over z, y_hi, x, core), harm: 2 (over y_lo).
Axes of the slice: x: 4, y: 4 (y_hi: 2, y_lo: 2; y = y_hi * 2 + y_lo), z: 8, core: 2. Of those that a mesh axis runs over, the one named last changes fastest.
Arguments:
- disp: float32 [128, 3, 64, 1024], P('sector', None, 'harm'), may hold values from -0.6 to 0.6
- direction: float32 [128, 3, 64, 1024], P('sector', None, 'harm'), may hold values from -0.6 to 0.6
- stick_state: int32 [128, 128, 1024], P('sector'), may hold values from 0 to 2
- contact_params: float32 [128, 4, 1024], P('sector'), may hold values from 0.3 to 3
- mistuning: float32 [128], replicated, may hold values from 1 to 4
- group_ids: int32 [128], replicated, may hold values from 0 to 31, never falling along the last dimension, each value on 1 to 8 neighbouring positions
- diag_stiff: float32 [64, 128], P('harm'), may hold values from 1 to 10
- cross_stiff: float32 [64, 128], P('harm'), may hold values from -3 to 3
- excitation: float32 [3, 64, 1024, 128], P(None, 'harm', 'sector'), may hold values from -1.8 to 1.8
Outputs:
- residual: float32 [3, 64, 1024, 128], P(None, 'harm', 'sector')
- jvp: float32 [3, 64, 1024, 128], P(None, 'harm', 'sector')
The draws below stay inside these ranges and needn't reach their ends.
Inputs may be any that keep to these rules, and one draw needn't show every extreme that they name: `group_ids`: the sectors of one group are consecutive and ids never fall; each of the 32 groups holds 1 to 8 sectors.
All inputs are finite; a program needn't handle non-finite values.
Results may differ from the reference program's by a relative error of at most 0.0003.
Values sent between devices are 32-bit elements; how exact they have to be, the bound alone decides.
No kernel may reach another device: no remote copies, remote signals or barrier semaphores. Data moves between devices by JAX's collectives and lax.ppermute only.
A program may use at most 64 MiB of HBM per device.

```python
import math
import jax
import jax.numpy as jnp
import numpy as np
from jax import lax

COEF = 64
SAMPLES = 128
CH = 3
NODES = 1024
SECTORS = 128
GROUPS = 32


def plant(result, key, smallest, high):
    longest = result.shape.index(max(result.shape))
    spots = []
    for shift in (0, 1):
        where = [jax.random.randint(jax.random.fold_in(key, axis), (), 0, length) for axis, length in enumerate(result.shape)]
        where[longest] = (where[longest] + shift) % result.shape[longest]
        spots.append(tuple(where))
    return result.at[spots[0]].set(smallest).at[spots[1]].set(high)


def block_levels(own_key, extent, split, smallest, high):
    factor_of = 1.0
    for position, parts in split:
        heights = jax.random.uniform(jax.random.fold_in(jax.random.fold_in(own_key, 6), position), (parts,), jnp.float32, smallest / len(split), high / len(split))
        factor_of = factor_of * jnp.repeat(jnp.exp(heights), extent[position] // parts).reshape((-1,) + (1,) * (len(extent) - 1 - position))
    return factor_of


def profile(amount, total, limit, skew):
    weights = [(1 << 20) // math.isqrt(standing ** skew) + 1 for standing in range(2, amount + 1)]
    surplus, given = total - limit - (amount - 1), [1] * (amount - 1)
    while surplus > 0:
        movable = [i for i in range(amount - 1) if given[i] < limit]
        whole, remaining = sum([weights[i] for i in movable]), surplus
        for i in movable:
            more = min(limit - given[i], max(1, remaining * weights[i] // whole), surplus)
            given[i] = given[i] + more
            surplus = surplus - more
    return np.array([limit] + given)


def uneven_parts(key, number_of, total, bound, skew):
    if number_of == 2:
        one = jax.random.randint(key, (), max(1, total - bound), min(bound, total - 1) + 1)
        return jnp.stack([one, total - one])
    sizes = jnp.asarray(profile(number_of, total, bound, skew), jnp.int32)
    pairs = (number_of - 1) // 2
    source_of, sink = sizes[1:1 + 2 * pairs:2], sizes[2:2 + 2 * pairs:2]
    slack = jnp.minimum(source_of - 1, bound - sink)
    passed = jax.random.randint(jax.random.fold_in(key, 1), (pairs,), 0, 1 << 20) % (slack + 1)
    sizes = sizes.at[1:1 + 2 * pairs:2].set(source_of - passed).at[2:2 + 2 * pairs:2].set(sink + passed)
    return sizes[jax.random.permutation(jax.random.fold_in(key, 2), number_of)]


def scatter_about(key, shape, spread, most, shards=(), kind=jnp.bfloat16):
    result = spread * jax.random.normal(key, shape, jnp.float32)
    if shards:
        result = result * block_levels(key, shape, shards, -0.22, 0.18)
    return jnp.clip(result, -most, most).astype(kind)


def setup_inputs(seed: int = 0) -> dict:
    seeds = jax.random.split(jax.random.key(seed), 10)
    disp = scatter_about(seeds[0], (SECTORS, CH, COEF, NODES), 0.1, 0.6, ((0, 128), (2, 2)), jnp.float32)
    direction = scatter_about(seeds[1], (SECTORS, CH, COEF, NODES), 0.1, 0.6, ((0, 128), (2, 2)), jnp.float32)
    stick_state = plant(jax.random.randint(seeds[2], (SECTORS, SAMPLES, NODES), 0, 3), jax.random.fold_in(seeds[2], 1), 0, 2).astype(jnp.int32)
    contact_params = jnp.clip(jnp.exp(math.log(3.0) - 2.3025851 * jax.random.uniform(seeds[3], (SECTORS, 4, NODES), jnp.float32) ** block_levels(seeds[3], (SECTORS, 4, NODES), ((0, 128),), -0.2, 0.2)), 0.3, 3.0)
    mistuning = jnp.clip(jnp.exp(jax.random.uniform(seeds[4], (SECTORS,), jnp.float32, math.log(1.0), math.log(4.0))), 1.0, 4.0)
    group_ids = jnp.searchsorted(jnp.cumsum(uneven_parts(seeds[5], GROUPS, SECTORS, 8, 2)), jnp.arange(SECTORS), side="right").astype(jnp.int32)
    diag_stiff = jnp.clip(jnp.exp(math.log(10.0) - 2.3025851 * jax.random.uniform(seeds[6], (COEF, SECTORS), jnp.float32) ** block_levels(seeds[6], (COEF, SECTORS), ((0, 2),), -0.2, 0.2)), 1.0, 10.0)
    cross_stiff = jnp.clip(jax.random.uniform(seeds[7], (COEF, SECTORS), jnp.float32, -3.0, 3.0) * block_levels(seeds[7], (COEF, SECTORS), ((0, 2),), -0.4, 0.0), -3.0, 3.0)
    excitation = scatter_about(seeds[8], (CH, COEF, NODES, SECTORS), 0.3, 1.8, ((1, 2), (2, 128)), jnp.float32)
    return dict(disp=disp, direction=direction, stick_state=stick_state, contact_params=contact_params, mistuning=mistuning, group_ids=group_ids, diag_stiff=diag_stiff, cross_stiff=cross_stiff, excitation=excitation)


exact_mode = lax.Precision.HIGHEST

def basis_table(coefs, samples):
    coef_index = lax.broadcasted_iota(jnp.int32, (coefs, samples), 0)
    time_index = lax.broadcasted_iota(jnp.int32, (coefs, samples), 1)
    harmonic = coef_index // 2 + 1
    phase = harmonic * time_index % samples
    angle = phase.astype(jnp.float32) * (2.0 * math.pi / samples)
    return jnp.where(coef_index % 2 == 0, jnp.cos(angle), jnp.sin(angle))

def contact_law(gaps, dgaps, states_here, params):
    preload = params[0]
    normal_stiff = params[1]
    tangent_stiff = params[2]
    friction_coef = params[3]
    touching = (states_here != 2).astype(jnp.float32)
    sliding = states_here == 1
    normal = (preload + normal_stiff * gaps[0]) * touching
    dnormal = normal_stiff * dgaps[0] * touching
    radius = jnp.sqrt(gaps[1] * gaps[1] + gaps[2] * gaps[2] + 1.0)
    projected = (gaps[1] * dgaps[1] + gaps[2] * dgaps[2]) / (radius * radius * radius)
    tractions = [normal]
    dtractions = [dnormal]
    for channel in (1, 2):
        stuck = tangent_stiff * gaps[channel]
        dstuck = tangent_stiff * dgaps[channel]
        slipped = friction_coef * normal * gaps[channel] / radius
        dslipped = friction_coef * (dnormal * gaps[channel] / radius + normal * (dgaps[channel] / radius - gaps[channel] * projected))
        tractions.append(jnp.where(sliding, slipped, stuck) * touching)
        dtractions.append(jnp.where(sliding, dslipped, dstuck) * touching)
    return (jnp.stack(tractions), jnp.stack(dtractions))

def hartley(field):

    def per_channel(block):
        spectrum = jnp.fft.fft(block, axis=0)
        return jnp.transpose((spectrum.real - spectrum.imag) / math.sqrt(SECTORS), (1, 2, 0))
    return lax.map(per_channel, jnp.moveaxis(field, 1, 0))

def mirror(field):
    return jnp.roll(jnp.flip(field, -1), 1, -1)

def group_mean(field, group_ids):
    counts = jax.ops.segment_sum(jnp.ones((SECTORS,), jnp.float32), group_ids, num_segments=GROUPS)
    sums = jax.ops.segment_sum(field, group_ids, num_segments=GROUPS)
    return sums[group_ids] / counts[group_ids][:, None, None, None]

def reference(disp, direction, stick_state, contact_params, mistuning, group_ids, diag_stiff, cross_stiff, excitation):
    table = basis_table(COEF, SAMPLES)
    rel_disp = disp - jnp.roll(disp, -1, axis=0)
    rel_dir = direction - jnp.roll(direction, -1, axis=0)
    scale = 2.0 / SAMPLES

    def one_sector(items):
        rel_one, drel_one, states_one, params_one = items
        gaps = jnp.einsum('cjp,jt->ctp', rel_one, table, precision=exact_mode)
        dgaps = jnp.einsum('cjp,jt->ctp', drel_one, table, precision=exact_mode)
        traction, dtraction = contact_law(gaps, dgaps, states_one, params_one)
        load_one = jnp.einsum('ctp,jt->cjp', traction, table, precision=exact_mode) * scale
        dload_one = jnp.einsum('ctp,jt->cjp', dtraction, table, precision=exact_mode) * scale
        return (load_one, dload_one)
    loads, dloads = lax.map(one_sector, (rel_disp, rel_dir, stick_state, contact_params))
    weight = mistuning[:, None, None, None]
    force = loads - jnp.roll(loads, 1, axis=0) + weight * (disp - group_mean(disp, group_ids))
    dforce = dloads - jnp.roll(dloads, 1, axis=0) + weight * (direction - group_mean(direction, group_ids))
    stiff_diag = diag_stiff[None, :, None, :]
    stiff_cross = cross_stiff[None, :, None, :]
    disp_hat = hartley(disp)
    residual = stiff_diag * disp_hat + stiff_cross * mirror(disp_hat) + hartley(force) - excitation
    dir_hat = hartley(direction)
    jvp = stiff_diag * dir_hat + stiff_cross * mirror(dir_hat) + hartley(dforce)
    return (residual, jvp)
```

```python
import math

import jax
import jax.numpy as jnp
import ml_dtypes
import numpy as np
from jax import lax
from jax.experimental import pallas as pl
from jax.experimental.pallas import tpu as pltpu
from jax.sharding import PartitionSpec as P

F32 = jnp.float32
BF16 = jnp.bfloat16
N = 128
HALF = 32
ROWS = 9


def split_np(table):
    hi = table.astype(ml_dtypes.bfloat16)
    lo = (table - hi.astype(np.float64)).astype(ml_dtypes.bfloat16)
    return hi, lo


def tables():
    t = np.arange(N)
    j = np.arange(64) // 2 + 1
    angle = 2 * np.pi * (j[:, None] * t[None, :] % N) / N
    basis = np.where(np.arange(64)[:, None] % 2 == 0, np.cos(angle), np.sin(angle))
    angle = 2 * np.pi * (t[:, None] * t[None, :] % N) / N
    hart = (np.cos(angle) + np.sin(angle)) / math.sqrt(N)
    hart_mirror = (np.cos(angle) - np.sin(angle)) / math.sqrt(N)
    hart_diff = hart - np.roll(hart, -1, axis=0)
    hi, lo = split_np(basis.T)
    to_time = np.concatenate([hi, hi, lo], 1)
    hi, lo = split_np(basis * (2.0 / N))
    to_coef = np.concatenate([hi, hi, lo], 1)
    hi, lo = split_np(hart_diff)
    diff = np.concatenate([hi, hi, lo], 0)
    hi, lo = split_np(np.concatenate([hart, hart_mirror], 1))
    pair = np.concatenate([hi, hi, lo], 0)
    return to_time, to_coef, diff, pair, hart.astype(np.float32)


def halves(x):
    hi = x.astype(BF16)
    lo = (x - hi.astype(F32)).astype(BF16)
    return hi, lo


def mm(a, b):
    return jnp.dot(a, b, preferred_element_type=F32)


def pack_kernel(disp, direction, stick, params, out, scr0, scr1):
    h = lax.axis_index("harm")
    d = disp[0].reshape(96, N)
    e = direction[0].reshape(96, N)
    z = stick[0, pl.ds(pl.multiple_of(h * 64, 64), 64), :].astype(F32)
    scr0[...] = jnp.concatenate([d, e[:32]], 0).T
    scr1[...] = jnp.concatenate([e[32:], z], 0).T
    for i in range(4):
        out[pl.ds(2 * i, 32, stride=ROWS), :] = scr0[pl.ds(i, 32, stride=4), :]
        out[pl.ds(2 * i + 1, 32, stride=ROWS), :] = scr1[pl.ds(i, 32, stride=4), :]
    p = params[0]
    first = jnp.where(h == 0, p[0:1], p[2:3])
    second = pltpu.roll(jnp.where(h == 0, p[1:2], p[3:4]), 4, 1)
    lane = lax.broadcasted_iota(jnp.int32, (32, N), 1) // 4
    row = lax.broadcasted_iota(jnp.int32, (32, N), 0)
    out[pl.ds(8, 32, stride=ROWS), :] = jnp.where(lane == row, first, second)


def pack(disp, direction, stick, params):
    return pl.pallas_call(
        pack_kernel,
        grid=(8,),
        in_specs=[
            pl.BlockSpec((1, 3, 32, N), lambda g: (0, 0, 0, g)),
            pl.BlockSpec((1, 3, 32, N), lambda g: (0, 0, 0, g)),
            pl.BlockSpec((1, 128, N), lambda g: (0, 0, g)),
            pl.BlockSpec((1, 4, N), lambda g: (0, 0, g)),
        ],
        out_specs=pl.BlockSpec((32 * ROWS, N), lambda g: (g, 0)),
        out_shape=jax.ShapeDtypeStruct((256 * ROWS, N), F32),
        scratch_shapes=[pltpu.VMEM((N, N), F32), pltpu.VMEM((N, N), F32)],
        name="pack",
    )(disp, direction, stick, params)


def contact_kernel(
    got, stiff, other_stiff, mist, groups, to_time, to_coef, diff, pair, hart,
    mine, send, wide, tall, res,
):
    i = pl.program_id(0)
    h = lax.axis_index("harm")
    spot = (lax.axis_index("sector") * 2 + h) % 32

    @pl.when(i == 0)
    def _():
        for half in range(2):
            block = got[pl.ds(half * ROWS + 8, N, stride=2 * ROWS), :]
            block = pltpu.roll(block, (N - 4 * spot) % N, 1)
            tall[pl.ds(8 * half, 8), :] = block.T[0:8]
        here = jnp.broadcast_to(groups[...].astype(F32), (N, N))
        same = (here == here.T).astype(F32)
        members = jnp.sum(same, axis=0, keepdims=True)
        row = lax.broadcasted_iota(jnp.int32, (N, N), 0)
        lane = lax.broadcasted_iota(jnp.int32, (N, N), 1)
        pull = ((row == lane).astype(F32) - same / members) * mist[...]
        pulled = jnp.dot(pull, hart[...], preferred_element_type=F32,
                         precision=lax.Precision.HIGHEST)
        hi, lo = halves(pulled)
        wide[:, 0:256] = pair[...]
        wide[:, 256:384] = jnp.concatenate([hi, hi, lo], 0)

    parts = []
    for half in range(2):
        left = got[pl.ds(half * ROWS + 2 * i, N, stride=2 * ROWS), :].T
        right = got[pl.ds(half * ROWS + 2 * i + 1, N, stride=2 * ROWS), :].T
        parts.append((left, right))
    fields = []
    for q in range(6):
        side, at = (0, q) if q < 4 else (1, q - 4)
        fields.append(
            jnp.concatenate([p[side][32 * at : 32 * at + 32] for p in parts], 0)
        )
    state = jnp.concatenate([p[1][64:128] for p in parts], 0)
    x = jnp.concatenate(fields, 1)
    rel = jnp.concatenate([f - pltpu.roll(f, N - 1, 1) for f in fields], 1)
    hi, lo = halves(rel)
    gaps = mm(to_time[...], jnp.concatenate([hi, lo, hi], 0))
    g0, g1, g2, d0, d1, d2 = [gaps[:, N * q : N * q + N] for q in range(6)]
    n0 = tall[pl.ds(i, 1), :]
    kn = tall[pl.ds(4 + i, 1), :]
    kt = tall[pl.ds(8 + i, 1), :]
    mu = tall[pl.ds(12 + i, 1), :]
    touching = state < 1.5
    sliding = jnp.logical_and(state > 0.5, touching)
    sticking = state < 0.5
    normal = n0 + kn * g0
    dnormal = kn * d0
    inv = lax.rsqrt(g1 * g1 + g2 * g2 + 1.0)
    proj = (g1 * d1 + g2 * d2) * (inv * inv)
    u1 = g1 * inv
    u2 = g2 * inv
    force = mu * normal
    dforce = mu * dnormal
    zero = jnp.zeros_like(g0)
    gain = force * inv
    rate = dforce - force * proj
    out = [
        jnp.where(touching, normal, zero),
        jnp.where(sticking, kt * g1, jnp.where(sliding, force * u1, zero)),
        jnp.where(sticking, kt * g2, jnp.where(sliding, force * u2, zero)),
        jnp.where(touching, dnormal, zero),
        jnp.where(sticking, kt * d1, jnp.where(sliding, rate * u1 + gain * d1, zero)),
        jnp.where(sticking, kt * d2, jnp.where(sliding, rate * u2 + gain * d2, zero)),
    ]
    hi, lo = halves(jnp.concatenate(out, 1))
    load = mm(to_coef[...], jnp.concatenate([hi, lo, hi], 0))
    first = jnp.where(h == 0, stiff[...], other_stiff[...])
    second = jnp.where(h == 0, other_stiff[...], stiff[...])
    diag = jnp.concatenate([first[0], second[0]], 0)
    cross = jnp.concatenate([first[1], second[1]], 0)
    for q in range(6):
        hi, lo = halves(x[:, N * q : N * q + N])
        spec = mm(jnp.concatenate([hi, lo, hi], 1), wide[...])
        hi, lo = halves(load[:, N * q : N * q + N])
        total = mm(jnp.concatenate([hi, lo, hi], 1), diff[...])
        res[q] = (
            diag * spec[:, 0:N] + cross * spec[:, N : 2 * N] + spec[:, 2 * N :] + total
        )
    own = pl.multiple_of(h * HALF, HALF)
    other = pl.multiple_of((1 - h) * HALF, HALF)
    mine[...] = res[:, pl.ds(own, HALF), :].reshape(192, N)
    send[...] = res[:, pl.ds(other, HALF), :].reshape(192, N)


def contact(got, stiff, other_stiff, mist, groups):
    consts = tables()
    whole = lambda a: pl.BlockSpec(a.shape, lambda i: (0,) * a.ndim)
    args = (got, stiff, other_stiff, mist, groups) + consts
    return pl.pallas_call(
        contact_kernel,
        grid=(4,),
        in_specs=[whole(a) for a in args],
        out_specs=[pl.BlockSpec((192, N), lambda i: (i, 0))] * 2,
        out_shape=[jax.ShapeDtypeStruct((768, N), F32)] * 2,
        scratch_shapes=[
            pltpu.VMEM((384, 384), BF16),
            pltpu.VMEM((16, N), F32),
            pltpu.VMEM((6, 64, N), F32),
        ],
        name="contact",
    )(*args)


def place_kernel(mine, recv, exc, residual, jvp):
    h = lax.axis_index("harm")
    outs = (residual, jvp)
    for side in range(2):

        @pl.when(h == side)
        def _():
            for source, base in ((mine, 4 * side), (recv, 4 * (1 - side))):
                for w in range(2):
                    for ch in range(3):
                        for i in range(4):
                            rows = pl.ds(ch * 256 + base + i, 32, stride=8)
                            block = source[pl.ds((i * 6 + w * 3 + ch) * 32, 32), :]
                            if w == 0:
                                block = block - exc[rows, :]
                            outs[w][rows, :] = block


def place(mine, recv, exc):
    return pl.pallas_call(
        place_kernel,
        out_shape=[jax.ShapeDtypeStruct((768, N), F32)] * 2,
        name="place",
    )(mine, recv, exc)


def body(
    disp, direction, stick_state, contact_params, mistuning, group_ids,
    diag_stiff, cross_stiff, excitation,
):
    stiff = jnp.stack([diag_stiff, cross_stiff])
    other_stiff = lax.ppermute(stiff, "harm", [(0, 1), (1, 0)])
    packed = pack(disp, direction, stick_state, contact_params)
    got = lax.all_to_all(
        packed.reshape(256, 1, ROWS * N), ("sector", "harm"), 0, 0, tiled=True
    ).reshape(256 * ROWS, N)
    mine, send = contact(
        got, stiff, other_stiff, mistuning.reshape(1, N), group_ids.reshape(1, N)
    )
    recv = lax.ppermute(send, "harm", [(0, 1), (1, 0)])
    residual, jvp = place(mine, recv, excitation.reshape(768, N))
    shape = excitation.shape
    return residual.reshape(shape), jvp.reshape(shape)


def solution(mesh):
    in_specs = (
        P("sector", None, "harm", None),
        P("sector", None, "harm", None),
        P("sector", None, None),
        P("sector", None, None),
        P(),
        P(),
        P("harm", None),
        P("harm", None),
        P(None, "harm", "sector", None),
    )
    out_specs = (P(None, "harm", "sector", None), P(None, "harm", "sector", None))
    return jax.shard_map(body, mesh=mesh, in_specs=in_specs, out_specs=out_specs, check_vma=False)
```

```python
import functools
import math

import jax
import jax.numpy as jnp
import ml_dtypes
import numpy as np
from jax import lax
from jax.experimental import pallas as pl
from jax.experimental.pallas import tpu as pltpu
from jax.sharding import PartitionSpec as P

F32 = jnp.float32
BF16 = jnp.bfloat16
N = 128
HALF = 32
ROWS = 9


def split_np(table):
    hi = table.astype(ml_dtypes.bfloat16)
    lo = (table - hi.astype(np.float64)).astype(ml_dtypes.bfloat16)
    return hi, lo


def tables():
    t = np.arange(N)
    j = np.arange(64) // 2 + 1
    angle = 2 * np.pi * (j[:, None] * t[None, :] % N) / N
    basis = np.where(np.arange(64)[:, None] % 2 == 0, np.cos(angle), np.sin(angle))
    angle = 2 * np.pi * (t[:, None] * t[None, :] % N) / N
    hart = (np.cos(angle) + np.sin(angle)) / math.sqrt(N)
    hart_mirror = (np.cos(angle) - np.sin(angle)) / math.sqrt(N)
    hart_diff = hart - np.roll(hart, -1, axis=0)
    to_time, to_coef = [], []
    for h in range(2):
        own = np.roll(np.roll(basis, -32 * h, axis=0), -64 * h, axis=1)
        hi, lo = split_np(own.T)
        to_time.append(np.concatenate([hi, hi, lo], 1))
        hi, lo = split_np(own * (2.0 / N))
        to_coef.append(np.concatenate([hi, hi, lo], 1))
    hi, lo = split_np(hart_diff)
    diff = np.concatenate([hi, hi, lo], 0)
    hi, lo = split_np(np.concatenate([hart, hart_mirror], 1))
    pair = np.concatenate([hi, hi, lo], 0)
    return np.stack(to_time), np.stack(to_coef), diff, pair, hart.astype(np.float32)


def halves(x):
    hi = x.astype(BF16)
    lo = (x - hi.astype(F32)).astype(BF16)
    return hi, lo


def mm(a, b):
    return jnp.dot(a, b, preferred_element_type=F32)


def split_rows(x):
    hi, lo = halves(x)
    return jnp.concatenate([hi, lo, hi], 0)


def split_lanes(x):
    hi, lo = halves(x)
    return jnp.concatenate([hi, lo, hi], 1)


VM = pl.BlockSpec(memory_space=pltpu.VMEM)


def limits(megabytes):
    return pltpu.CompilerParams(vmem_limit_bytes=megabytes << 20)


def pack_kernel(disp, direction, stick, params, out, scr0, scr1):
    h = lax.axis_index("harm")
    for k in range(4):
        cols = pl.ds(k * N, N)
        d = disp[0, :, :, cols].reshape(96, N)
        e = direction[0, :, :, cols].reshape(96, N)
        z = stick[0, pl.ds(pl.multiple_of(h * 64, 64), 64), cols].astype(F32)
        scr0[k] = jnp.concatenate([d, e[:32]], 0).T
        scr1[k] = jnp.concatenate([e[32:], z], 0).T
        base = 32 * ROWS * k
        for i in range(4):
            to = pl.ds(base + 2 * i, 32, stride=ROWS)
            out[to, :] = scr0[k, pl.ds(i, 32, stride=4), :]
            to = pl.ds(base + 2 * i + 1, 32, stride=ROWS)
            out[to, :] = scr1[k, pl.ds(i, 32, stride=4), :]
        p = params[0, :, cols]
        first = jnp.where(h == 0, p[0:1], p[2:3])
        second = pltpu.roll(jnp.where(h == 0, p[1:2], p[3:4]), 4, 1)
        lane = lax.broadcasted_iota(jnp.int32, (32, N), 1) // 4
        row = lax.broadcasted_iota(jnp.int32, (32, N), 0)
        out[pl.ds(base + 8, 32, stride=ROWS), :] = jnp.where(lane == row, first, second)


def pack(disp, direction, stick, params):
    return pl.pallas_call(
        pack_kernel,
        grid=(2,),
        in_specs=[
            pl.BlockSpec((1, 3, 32, 4 * N), lambda g: (0, 0, 0, g)),
            pl.BlockSpec((1, 3, 32, 4 * N), lambda g: (0, 0, 0, g)),
            pl.BlockSpec((1, 128, 4 * N), lambda g: (0, 0, g)),
            pl.BlockSpec((1, 4, 4 * N), lambda g: (0, 0, g)),
        ],
        out_specs=pl.BlockSpec((128 * ROWS, N), lambda g: (g, 0)),
        out_shape=jax.ShapeDtypeStruct((256 * ROWS, N), F32),
        scratch_shapes=[pltpu.VMEM((4, N, N), F32), pltpu.VMEM((4, N, N), F32)],
        name="pack",
    )(disp, direction, stick, params)


def prep_kernel(mist, groups, pair, hart, wide):
    here = jnp.broadcast_to(groups[...].astype(F32), (N, N))
    same = (here == here.T).astype(F32)
    members = jnp.sum(same, axis=0, keepdims=True)
    row = lax.broadcasted_iota(jnp.int32, (N, N), 0)
    lane = lax.broadcasted_iota(jnp.int32, (N, N), 1)
    pull = ((row == lane).astype(F32) - same / members) * mist[...]
    pulled = jnp.dot(
        pull, hart[...], preferred_element_type=F32, precision=lax.Precision.HIGHEST
    )
    hi, lo = halves(pulled)
    wide[:, 0:256] = pair[...]
    wide[:, 256:384] = jnp.concatenate([hi, hi, lo], 0)


def prep(mist, groups, pair, hart):
    return pl.pallas_call(
        prep_kernel,
        in_specs=[VM] * 4,
        out_specs=VM,
        out_shape=jax.ShapeDtypeStruct((384, 384), BF16),
        compiler_params=limits(8),
        cost_estimate=pl.CostEstimate(flops=10**8, bytes_accessed=10**6, transcendentals=0),
        name="prep",
    )(mist, groups, pair, hart)


def contact_kernel(w, got, stiff, other, wide, to_time, to_coef, diff, mine, send):
    h = lax.axis_index("harm")
    spot = (lax.axis_index("sector") * 2 + h) % 32
    step = 2 * ROWS
    tall = []
    for half in range(2):
        block = got[pl.ds(half * ROWS + 8, N, stride=step), :]
        block = pltpu.roll(block, (N - 4 * spot) % N, 1).T
        for at in range(2):
            tall.append(
                jnp.concatenate([block[4 * at + i : 4 * at + i + 1] for i in range(4)], 1)
            )
    n0, kn, kt, mu = tall
    disp = [[], [], []]
    dirs = [[], [], []]
    state = []
    for i in range(4):
        parts = []
        for half in (h, 1 - h):
            left = got[pl.ds(half * ROWS + 2 * i, N, stride=step), :].T
            right = got[pl.ds(half * ROWS + 2 * i + 1, N, stride=step), :].T
            parts.append((left, right))
        for q in range(3 + 3 * w):
            side, at = (0, q) if q < 4 else (1, q - 4)
            field = [p[side][32 * at : 32 * at + 32] for p in parts]
            (disp if q < 3 else dirs)[q % 3].append(jnp.concatenate(field, 0))
        state.append(jnp.concatenate([p[1][64:128] for p in parts], 0))
    state = jnp.concatenate(state, 1)
    wave = to_time[h]

    def gap_of(fields):
        rel = [f - pltpu.roll(f, N - 1, 1) for ch in fields for f in ch]
        out = mm(wave, split_rows(jnp.concatenate(rel, 1)))
        return [out[:, 512 * ch : 512 * ch + 512] for ch in range(3)]

    g0, g1, g2 = gap_of(disp)
    touching = state < 1.5
    sticking = state < 0.5
    normal = n0 + kn * g0
    inv = lax.rsqrt(g1 * g1 + g2 * g2 + 1.0)
    zero = jnp.zeros_like(g0)
    gain = mu * normal * inv
    if w == 0:
        coef = jnp.where(sticking, kt, jnp.where(touching, gain, zero))
        out = [jnp.where(touching, normal, zero), coef * g1, coef * g2]
        fields = disp
    else:
        d0, d1, d2 = gap_of(dirs)
        dnormal = kn * d0
        proj = (g1 * d1 + g2 * d2) * (inv * inv)
        rate = mu * dnormal * inv - gain * proj
        coef = jnp.where(sticking, kt, jnp.where(touching, gain, zero))
        rate = jnp.where(sticking, zero, jnp.where(touching, rate, zero))
        out = [
            jnp.where(touching, dnormal, zero),
            coef * d1 + rate * g1,
            coef * d2 + rate * g2,
        ]
        fields = dirs
    load = mm(to_coef[h], split_rows(jnp.concatenate(out, 1)))
    load = jnp.concatenate([load[:, N * q : N * q + N] for q in range(12)], 0)
    x = jnp.concatenate([f for ch in fields for f in ch], 0)
    spec = mm(split_lanes(x), wide[...])
    total = mm(split_lanes(load), diff[...])
    diag = jnp.concatenate([stiff[0], other[0]], 0)
    cross = jnp.concatenate([stiff[1], other[1]], 0)
    for q in range(12):
        rows = slice(64 * q, 64 * q + 64)
        res = (
            diag * spec[rows, 0:N] + cross * spec[rows, N : 2 * N]
            + spec[rows, 2 * N :] + total[rows]
        )
        mine[32 * q : 32 * q + 32, :] = res[0:32]
        send[32 * q : 32 * q + 32, :] = res[32:64]


def contact(w, *args):
    return pl.pallas_call(
        functools.partial(contact_kernel, w),
        in_specs=[VM] * len(args),
        out_specs=[VM] * 2,
        out_shape=[jax.ShapeDtypeStruct((384, N), F32)] * 2,
        compiler_params=limits(32),
        cost_estimate=pl.CostEstimate(flops=10**9, bytes_accessed=4 * 10**6, transcendentals=0),
        name="jvp" if w else "residual",
    )(*args)


def place_kernel(mine, recv, *refs):
    h = lax.axis_index("harm")
    out = refs[-1]
    for side in range(2):

        @pl.when(h == side)
        def _():
            for source, base in ((mine, 4 * side), (recv, 4 * (1 - side))):
                for ch in range(3):
                    for i in range(4):
                        rows = pl.ds(ch * 256 + base + i, 32, stride=8)
                        block = source[pl.ds((ch * 4 + i) * 32, 32), :]
                        if len(refs) == 2:
                            block = block - refs[0][rows, :]
                        out[rows, :] = block


def place(name, *args):
    return pl.pallas_call(
        place_kernel,
        in_specs=[VM] * len(args),
        out_specs=VM,
        out_shape=jax.ShapeDtypeStruct((768, N), F32),
        compiler_params=limits(8),
        cost_estimate=pl.CostEstimate(flops=10**6, bytes_accessed=2 * 10**6, transcendentals=0),
        name=name,
    )(*args)


def swap(x):
    return lax.ppermute(x, "harm", [(0, 1), (1, 0)])


def body(
    disp, direction, stick_state, contact_params, mistuning, group_ids,
    diag_stiff, cross_stiff, excitation,
):
    to_time, to_coef, diff, pair, hart = tables()
    stiff = jnp.stack([diag_stiff, cross_stiff])
    other = swap(stiff)
    packed = pack(disp, direction, stick_state, contact_params)
    got = lax.all_to_all(
        packed.reshape(256, 1, ROWS * N), ("sector", "harm"), 0, 0, tiled=True
    ).reshape(256 * ROWS, N)
    wide = prep(mistuning.reshape(1, N), group_ids.reshape(1, N), pair, hart)
    args = (stiff, other, wide, to_time, to_coef, diff)
    mine0, send0 = contact(0, got, *args)
    send0, got = lax.optimization_barrier((send0, got))
    recv0 = swap(send0)
    mine1, send1 = contact(1, got, *args)
    recv1 = swap(send1)
    shape = excitation.shape
    residual = place("place0", mine0, recv0, excitation.reshape(768, N))
    mine1, residual = lax.optimization_barrier((mine1, residual))
    jvp = place("place1", mine1, recv1)
    return residual.reshape(shape), jvp.reshape(shape)


def solution(mesh):
    in_specs = (
        P("sector", None, "harm", None),
        P("sector", None, "harm", None),
        P("sector", None, None),
        P("sector", None, None),
        P(),
        P(),
        P("harm", None),
        P("harm", None),
        P(None, "harm", "sector", None),
    )
    out_specs = (P(None, "harm", "sector", None), P(None, "harm", "sector", None))
    return jax.shard_map(body, mesh=mesh, in_specs=in_specs, out_specs=out_specs, check_vma=False)
```

```python
import functools
import math

import jax
import jax.numpy as jnp
import ml_dtypes
import numpy as np
from jax import lax
from jax.experimental import pallas as pl
from jax.experimental.pallas import tpu as pltpu
from jax.sharding import PartitionSpec as P

F32 = jnp.float32
BF16 = jnp.bfloat16
N = 128
HALF = 32
ROWS = 9


def split_np(table):
    hi = table.astype(ml_dtypes.bfloat16)
    lo = (table - hi.astype(np.float64)).astype(ml_dtypes.bfloat16)
    return hi, lo


def tables():
    t = np.arange(N)
    j = np.arange(64) // 2 + 1
    angle = 2 * np.pi * (j[:, None] * t[None, :] % N) / N
    basis = np.where(np.arange(64)[:, None] % 2 == 0, np.cos(angle), np.sin(angle))
    angle = 2 * np.pi * (t[:, None] * t[None, :] % N) / N
    hart = (np.cos(angle) + np.sin(angle)) / math.sqrt(N)
    hart_mirror = (np.cos(angle) - np.sin(angle)) / math.sqrt(N)
    hart_diff = hart - np.roll(hart, -1, axis=0)
    to_time, to_coef = [], []
    for h in range(2):
        own = np.roll(np.roll(basis, -32 * h, axis=0), -64 * h, axis=1)
        hi, lo = split_np(own.T)
        to_time.append(np.concatenate([hi, hi, lo], 1))
        hi, lo = split_np(own * (2.0 / N))
        to_coef.append(np.concatenate([hi, hi, lo], 1))
    hi, lo = split_np(hart_diff)
    diff = np.concatenate([hi, hi, lo], 0)
    hi, lo = split_np(np.concatenate([hart, hart_mirror], 1))
    pair = np.concatenate([hi, hi, lo], 0)
    return np.stack(to_time), np.stack(to_coef), diff, pair, hart.astype(np.float32)


def halves(x):
    hi = x.astype(BF16)
    lo = (x - hi.astype(F32)).astype(BF16)
    return hi, lo


def mm(a, b):
    return jnp.dot(a, b, preferred_element_type=F32)


def split_rows(x):
    hi, lo = halves(x)
    return jnp.concatenate([hi, lo, hi], 0)


def split_lanes(x):
    hi, lo = halves(x)
    return jnp.concatenate([hi, lo, hi], 1)


VM = pl.BlockSpec(memory_space=pltpu.VMEM)


def limits(megabytes):
    return pltpu.CompilerParams(vmem_limit_bytes=megabytes << 20)


def pack_kernel(disp, direction, stick, params, out, scr0, scr1):
    h = lax.axis_index("harm")
    for k in range(4):
        cols = pl.ds(k * N, N)
        d = disp[0, :, :, cols].reshape(96, N)
        e = direction[0, :, :, cols].reshape(96, N)
        z = stick[0, pl.ds(pl.multiple_of(h * 64, 64), 64), cols].astype(F32)
        scr0[k] = jnp.concatenate([d, e[:32]], 0).T
        scr1[k] = jnp.concatenate([e[32:], z], 0).T
        base = 32 * ROWS * k
        for i in range(4):
            to = pl.ds(base + 2 * i, 32, stride=ROWS)
            out[to, :] = scr0[k, pl.ds(i, 32, stride=4), :]
            to = pl.ds(base + 2 * i + 1, 32, stride=ROWS)
            out[to, :] = scr1[k, pl.ds(i, 32, stride=4), :]
        p = params[0, :, cols]
        first = jnp.where(h == 0, p[0:1], p[2:3])
        second = pltpu.roll(jnp.where(h == 0, p[1:2], p[3:4]), 4, 1)
        lane = lax.broadcasted_iota(jnp.int32, (32, N), 1) // 4
        row = lax.broadcasted_iota(jnp.int32, (32, N), 0)
        out[pl.ds(base + 8, 32, stride=ROWS), :] = jnp.where(lane == row, first, second)


def pack(disp, direction, stick, params):
    return pl.pallas_call(
        pack_kernel,
        grid=(2,),
        in_specs=[
            pl.BlockSpec((1, 3, 32, 4 * N), lambda g: (0, 0, 0, g)),
            pl.BlockSpec((1, 3, 32, 4 * N), lambda g: (0, 0, 0, g)),
            pl.BlockSpec((1, 128, 4 * N), lambda g: (0, 0, g)),
            pl.BlockSpec((1, 4, 4 * N), lambda g: (0, 0, g)),
        ],
        out_specs=pl.BlockSpec((128 * ROWS, N), lambda g: (g, 0)),
        out_shape=jax.ShapeDtypeStruct((256 * ROWS, N), F32),
        scratch_shapes=[pltpu.VMEM((4, N, N), F32), pltpu.VMEM((4, N, N), F32)],
        name="pack",
    )(disp, direction, stick, params)


def prep_kernel(mist, groups, pair, hart, wide):
    here = jnp.broadcast_to(groups[...].astype(F32), (N, N))
    same = (here == here.T).astype(F32)
    members = jnp.sum(same, axis=0, keepdims=True)
    row = lax.broadcasted_iota(jnp.int32, (N, N), 0)
    lane = lax.broadcasted_iota(jnp.int32, (N, N), 1)
    pull = ((row == lane).astype(F32) - same / members) * mist[...]
    pulled = jnp.dot(
        pull, hart[...], preferred_element_type=F32, precision=lax.Precision.HIGHEST
    )
    hi, lo = halves(pulled)
    wide[:, 0:256] = pair[...]
    wide[:, 256:384] = jnp.concatenate([hi, hi, lo], 0)


def prep(mist, groups, pair, hart):
    return pl.pallas_call(
        prep_kernel,
        in_specs=[VM] * 4,
        out_specs=VM,
        out_shape=jax.ShapeDtypeStruct((384, 384), BF16),
        compiler_params=limits(8),
        cost_estimate=pl.CostEstimate(flops=10**8, bytes_accessed=10**6, transcendentals=0),
        name="prep",
    )(mist, groups, pair, hart)


def contact_kernel(
    fields, part, got, stiff, wide, to_time, to_coef, diff, *outs
):
    h = lax.axis_index("harm")
    spot = (lax.axis_index("sector") * 2 + h) % 32
    step = 2 * ROWS
    tall = []
    for half in range(2):
        block = got[pl.ds(half * ROWS + 8, N, stride=step), :]
        block = pltpu.roll(block, (N - 4 * spot) % N, 1).T
        for at in range(2):
            tall.append(
                jnp.concatenate([block[4 * at + i : 4 * at + i + 1] for i in range(4)], 1)
            )
    n0, kn, kt, mu = tall
    states = [[[], [], []], [[], [], []]]
    stick = []
    for i in range(4):
        parts = []
        for half in (h, 1 - h):
            left = got[pl.ds(half * ROWS + 2 * i, N, stride=step), :].T
            right = got[pl.ds(half * ROWS + 2 * i + 1, N, stride=step), :].T
            parts.append((left, right))
        for q in range(3 + 3 * max(fields)):
            side, at = (0, q) if q < 4 else (1, q - 4)
            coefs = [p[side][HALF * at : HALF * at + HALF] for p in parts]
            states[q // 3][q % 3].append(coefs)
        stick.append(jnp.concatenate([p[1][64:128] for p in parts], 0))
    stick = jnp.concatenate(stick, 1)
    wave = to_time[h]

    def gap_of(state):
        all_coefs = [jnp.concatenate(c, 0) for ch in state for c in ch]
        rel = [f - pltpu.roll(f, N - 1, 1) for f in all_coefs]
        out = mm(wave, split_rows(jnp.concatenate(rel, 1)))
        return jnp.split(out, 3, axis=1)

    g0, g1, g2 = gap_of(states[0])
    touching = stick < 1.5
    sticking = stick < 0.5
    normal = n0 + kn * g0
    inv = lax.rsqrt(g1 * g1 + g2 * g2 + 1.0)
    zero = jnp.zeros_like(g0)
    gain = mu * normal * inv
    coef = jnp.where(sticking, kt, jnp.where(touching, gain, zero))
    for w, out in zip(fields, outs):
        if w == 0:
            traction = [jnp.where(touching, normal, zero), coef * g1, coef * g2]
        else:
            d0, d1, d2 = gap_of(states[1])
            dnormal = kn * d0
            proj = (g1 * d1 + g2 * d2) * (inv * inv)
            rate = mu * dnormal * inv - gain * proj
            rate = jnp.where(sticking, zero, jnp.where(touching, rate, zero))
            traction = [
                jnp.where(touching, dnormal, zero),
                coef * d1 + rate * g1,
                coef * d2 + rate * g2,
            ]
        weights = to_coef[h, HALF * part : HALF * part + HALF]
        load = mm(weights, split_rows(jnp.concatenate(traction, 1)))
        load = jnp.concatenate([load[:, N * q : N * q + N] for q in range(12)], 0)
        x = jnp.concatenate([c[part] for ch in states[w] for c in ch], 0)
        spec = mm(split_lanes(x), wide[...])
        total = mm(split_lanes(load), diff[...])
        for q in range(12):
            rows = slice(HALF * q, HALF * q + HALF)
            out[rows, :] = (
                stiff[0] * spec[rows, 0:N] + stiff[1] * spec[rows, N : 2 * N]
                + spec[rows, 2 * N :] + total[rows]
            )


def contact(name, fields, part, *args):
    return pl.pallas_call(
        functools.partial(contact_kernel, fields, part),
        in_specs=[VM] * len(args),
        out_specs=[VM] * len(fields),
        out_shape=[jax.ShapeDtypeStruct((384, N), F32)] * len(fields),
        compiler_params=limits(32),
        cost_estimate=pl.CostEstimate(
            flops=10**9 * len(fields), bytes_accessed=2 * 10**6, transcendentals=0
        ),
        name=name,
    )(*args)


def place_kernel(mine, recv, *refs):
    h = lax.axis_index("harm")
    out = refs[-1]
    for side in range(2):

        @pl.when(h == side)
        def _():
            for source, base in ((mine, 4 * side), (recv, 4 * (1 - side))):
                for ch in range(3):
                    for i in range(4):
                        rows = pl.ds(ch * 256 + base + i, 32, stride=8)
                        block = source[pl.ds((ch * 4 + i) * 32, 32), :]
                        if len(refs) == 2:
                            block = block - refs[0][rows, :]
                        out[rows, :] = block


def place(name, *args):
    return pl.pallas_call(
        place_kernel,
        in_specs=[VM] * len(args),
        out_specs=VM,
        out_shape=jax.ShapeDtypeStruct((768, N), F32),
        compiler_params=limits(8),
        cost_estimate=pl.CostEstimate(flops=10**6, bytes_accessed=2 * 10**6, transcendentals=0),
        name=name,
    )(*args)


def swap(x):
    return lax.ppermute(x, "harm", [(0, 1), (1, 0)])


def body(
    disp, direction, stick_state, contact_params, mistuning, group_ids,
    diag_stiff, cross_stiff, excitation,
):
    to_time, to_coef, diff, pair, hart = tables()
    stiff = jnp.stack([diag_stiff, cross_stiff])
    other = swap(stiff)
    packed = pack(disp, direction, stick_state, contact_params)
    got = lax.all_to_all(
        packed.reshape(256, 1, ROWS * N), ("sector", "harm"), 0, 0, tiled=True
    ).reshape(256 * ROWS, N)
    wide = prep(mistuning.reshape(1, N), group_ids.reshape(1, N), pair, hart)
    args = (wide, to_time, to_coef, diff)
    (send0,) = contact("send0", (0,), 1, got, other, *args)
    send0, got = lax.optimization_barrier((send0, got))
    recv0 = swap(send0)
    (send1,) = contact("send1", (1,), 1, got, other, *args)
    send1, got = lax.optimization_barrier((send1, got))
    recv1 = swap(send1)
    mine0, mine1 = contact("keep", (0, 1), 0, got, stiff, *args)
    shape = excitation.shape
    residual = place("place0", mine0, recv0, excitation.reshape(768, N))
    mine1, residual = lax.optimization_barrier((mine1, residual))
    jvp = place("place1", mine1, recv1)
    return residual.reshape(shape), jvp.reshape(shape)


def solution(mesh):
    in_specs = (
        P("sector", None, "harm", None),
        P("sector", None, "harm", None),
        P("sector", None, None),
        P("sector", None, None),
        P(),
        P(),
        P("harm", None),
        P("harm", None),
        P(None, "harm", "sector", None),
    )
    out_specs = (P(None, "harm", "sector", None), P(None, "harm", "sector", None))
    return jax.shard_map(body, mesh=mesh, in_specs=in_specs, out_specs=out_specs, check_vma=False)
```

```python
import functools
import math

import jax
import jax.numpy as jnp
import ml_dtypes
import numpy as np
from jax import lax
from jax.experimental import pallas as pl
from jax.experimental.pallas import tpu as pltpu
from jax.sharding import PartitionSpec as P

F32 = jnp.float32
BF16 = jnp.bfloat16
N = 128
HALF = 32
PARTS = 2
WIDE = 1024 // PARTS
ROWS = 9


def split_np(table):
    hi = table.astype(ml_dtypes.bfloat16)
    lo = (table - hi.astype(np.float64)).astype(ml_dtypes.bfloat16)
    return hi, lo


def tables():
    t = np.arange(N)
    j = np.arange(64) // 2 + 1
    angle = 2 * np.pi * (j[:, None] * t[None, :] % N) / N
    basis = np.where(np.arange(64)[:, None] % 2 == 0, np.cos(angle), np.sin(angle))
    angle = 2 * np.pi * (t[:, None] * t[None, :] % N) / N
    hart = (np.cos(angle) + np.sin(angle)) / math.sqrt(N)
    hart_mirror = (np.cos(angle) - np.sin(angle)) / math.sqrt(N)
    hart_diff = hart - np.roll(hart, -1, axis=0)
    to_time, to_coef = [], []
    for h in range(2):
        own = np.roll(np.roll(basis, -32 * h, axis=0), -64 * h, axis=1)
        hi, lo = split_np(own.T)
        to_time.append(np.concatenate([hi, hi, lo], 1))
        hi, lo = split_np(own * (2.0 / N))
        to_coef.append(np.concatenate([hi, hi, lo], 1))
    hi, lo = split_np(hart_diff)
    diff = np.concatenate([hi, hi, lo], 0)
    hi, lo = split_np(np.concatenate([hart, hart_mirror], 1))
    pair = np.concatenate([hi, hi, lo], 0)
    return np.stack(to_time), np.stack(to_coef), diff, pair, hart.astype(np.float32)


def halves(x):
    hi = x.astype(BF16)
    lo = (x - hi.astype(F32)).astype(BF16)
    return hi, lo


def mm(a, b):
    return jnp.dot(a, b, preferred_element_type=F32)


def split_rows(x):
    hi, lo = halves(x)
    return jnp.concatenate([hi, lo, hi], 0)


def split_lanes(x):
    hi, lo = halves(x)
    return jnp.concatenate([hi, lo, hi], 1)


VM = pl.BlockSpec(memory_space=pltpu.VMEM)


def limits(megabytes):
    return pltpu.CompilerParams(vmem_limit_bytes=megabytes << 20)


def pack_kernel(
    disp, direction, stick, *refs
):
    small_hbm, (packed, wide, vd, ve, vz), refs = refs[:7], refs[7:12], refs[12:]
    small, (scr0, scr1, turned, sem, small_sem) = refs[:7], refs[7:]
    params, diag, cross, mist, groups, pair, hart = small
    h = lax.axis_index("harm")
    samples = pl.ds(pl.multiple_of(h * 64, 64), 64)
    copies, first = [], []
    for k in (3, 4, 6, 1, 2, 5, 0):
        first.append(pltpu.make_async_copy(small_hbm[k], small[k], small_sem.at[k]))
        first[-1].start()
    for g in range(PARTS):
        cols = pl.ds(g * WIDE, WIDE)
        copies.append(
            [
                pltpu.make_async_copy(disp.at[0, :, :, cols], vd.at[g], sem.at[g, 0]),
                pltpu.make_async_copy(direction.at[0, :, :, cols], ve.at[g], sem.at[g, 1]),
                pltpu.make_async_copy(stick.at[0, samples, cols], vz.at[g], sem.at[g, 2]),
            ]
        )
        for copy in copies[-1]:
            copy.start()

    for copy in first:
        copy.wait()
    here = jnp.broadcast_to(groups[...].astype(F32), (N, N))
    same = (here == here.T).astype(F32)
    members = jnp.sum(same, axis=0, keepdims=True)
    row = lax.broadcasted_iota(jnp.int32, (N, N), 0)
    lane = lax.broadcasted_iota(jnp.int32, (N, N), 1)
    pull = ((row == lane).astype(F32) - same / members) * mist[...]
    pulled = jnp.dot(
        pull, hart[...], preferred_element_type=F32, precision=lax.Precision.HIGHEST
    )
    hi, lo = halves(pulled)
    wide[:, 0:256] = pair[...]
    wide[:, 256:384] = jnp.concatenate([hi, hi, lo], 0)

    turned[...] = jnp.concatenate([diag[...], cross[...]] * 2, 0).T
    column = turned[pl.ds(lax.axis_index("sector"), 1), :]
    column = jnp.broadcast_to(pltpu.roll(column, 8, 1), (32, N))
    column = pltpu.roll(column, 0, 1, stride=4, stride_axis=0)
    spot = lax.broadcasted_iota(jnp.int32, (32, N), 0)
    quad = lax.broadcasted_iota(jnp.int32, (32, N), 1) // 4
    for k in range(8):
        g, at = divmod(k * N, WIDE)
        if at == 0:
            for copy in copies[g]:
                copy.wait()
        cols = pl.ds(at, N)
        d = vd[g, :, :, cols].reshape(96, N)
        e = ve[g, :, :, cols].reshape(96, N)
        z = vz[g, :, cols].astype(F32)
        scr0[k] = jnp.concatenate([d, e[:32]], 0).T
        scr1[k] = jnp.concatenate([e[32:], z], 0).T
        base = 32 * ROWS * k
        for i in range(4):
            to = pl.ds(base + 2 * i, 32, stride=ROWS)
            packed[to, :] = scr0[k, pl.ds(i, 32, stride=4), :]
            to = pl.ds(base + 2 * i + 1, 32, stride=ROWS)
            packed[to, :] = scr1[k, pl.ds(i, 32, stride=4), :]
        p = params[0, :, pl.ds(k * N, N)]
        near = jnp.where(h == 0, p[0:1], p[2:3])
        second = pltpu.roll(jnp.where(h == 0, p[1:2], p[3:4]), 4, 1)
        last = jnp.where(quad == (spot + 1) % 32, second, column)
        packed[pl.ds(base + 8, 32, stride=ROWS), :] = jnp.where(quad == spot, near, last)


def pack(*args):
    return pl.pallas_call(
        pack_kernel,
        in_specs=[pl.BlockSpec(memory_space=pl.ANY)] * len(args),
        out_specs=[VM, VM],
        out_shape=[
            jax.ShapeDtypeStruct((256 * ROWS, N), F32),
            jax.ShapeDtypeStruct((384, 384), BF16),
        ],
        scratch_shapes=[
            pltpu.VMEM((PARTS, 3, 32, WIDE), F32),
            pltpu.VMEM((PARTS, 3, 32, WIDE), F32),
            pltpu.VMEM((PARTS, 64, WIDE), jnp.int32),
        ]
        + [pltpu.VMEM(a.shape, a.dtype) for a in args[3:]]
        + [
            pltpu.VMEM((8, N, N), F32),
            pltpu.VMEM((8, N, N), F32),
            pltpu.VMEM((N, N), F32),
            pltpu.SemaphoreType.DMA((PARTS, 3)),
            pltpu.SemaphoreType.DMA((7,)),
        ],
        compiler_params=limits(40),
        name="pack",
    )(*[pltpu.with_memory_space_constraint(a, pltpu.HBM) for a in args])


def contact_kernel(
    fields, part, got, wide, to_time, to_coef, diff, *outs
):
    h = lax.axis_index("harm")
    spot = (lax.axis_index("sector") * 2 + h) % 32
    step = 2 * ROWS
    tall, stiff = [], []
    for half in range(2):
        block = got[pl.ds(half * ROWS + 8, N, stride=step), :]
        block = pltpu.roll(block, (N - 4 * spot) % N, 1).T
        for at in range(2):
            tall.append(
                jnp.concatenate([block[4 * at + i : 4 * at + i + 1] for i in range(4)], 1)
            )
        stiff.append(block[8:72])
    stiff = jnp.where(h == part, stiff[0], stiff[1])
    diag, cross = stiff[0:HALF], stiff[HALF:64]
    n0, kn, kt, mu = tall
    states = [[[], [], []], [[], [], []]]
    stick = []
    for i in range(4):
        parts = []
        for half in (h, 1 - h):
            left = got[pl.ds(half * ROWS + 2 * i, N, stride=step), :].T
            right = got[pl.ds(half * ROWS + 2 * i + 1, N, stride=step), :].T
            parts.append((left, right))
        for q in range(3 + 3 * max(fields)):
            side, at = (0, q) if q < 4 else (1, q - 4)
            coefs = [p[side][HALF * at : HALF * at + HALF] for p in parts]
            states[q // 3][q % 3].append(coefs)
        stick.append(jnp.concatenate([p[1][64:128] for p in parts], 0))
    stick = jnp.concatenate(stick, 1)
    wave = to_time[h]

    def gap_of(state):
        all_coefs = [jnp.concatenate(c, 0) for ch in state for c in ch]
        rel = [f - pltpu.roll(f, N - 1, 1) for f in all_coefs]
        out = mm(wave, split_rows(jnp.concatenate(rel, 1)))
        return jnp.split(out, 3, axis=1)

    g0, g1, g2 = gap_of(states[0])
    touching = stick < 1.5
    sticking = stick < 0.5
    normal = n0 + kn * g0
    inv = lax.rsqrt(g1 * g1 + g2 * g2 + 1.0)
    zero = jnp.zeros_like(g0)
    gain = mu * normal * inv
    coef = jnp.where(sticking, kt, jnp.where(touching, gain, zero))
    for w, out in zip(fields, outs):
        if w == 0:
            traction = [jnp.where(touching, normal, zero), coef * g1, coef * g2]
        else:
            d0, d1, d2 = gap_of(states[1])
            dnormal = kn * d0
            proj = (g1 * d1 + g2 * d2) * (inv * inv)
            rate = mu * dnormal * inv - gain * proj
            rate = jnp.where(sticking, zero, jnp.where(touching, rate, zero))
            traction = [
                jnp.where(touching, dnormal, zero),
                coef * d1 + rate * g1,
                coef * d2 + rate * g2,
            ]
        weights = to_coef[h, HALF * part : HALF * part + HALF]
        load = mm(weights, split_rows(jnp.concatenate(traction, 1)))
        load = jnp.concatenate([load[:, N * q : N * q + N] for q in range(12)], 0)
        x = jnp.concatenate([c[part] for ch in states[w] for c in ch], 0)
        spec = mm(split_lanes(x), wide[...])
        total = mm(split_lanes(load), diff[...])
        for q in range(12):
            rows = slice(HALF * q, HALF * q + HALF)
            out[rows, :] = (
                diag * spec[rows, 0:N] + cross * spec[rows, N : 2 * N]
                + spec[rows, 2 * N :] + total[rows]
            )


def contact(name, fields, part, *args):
    return pl.pallas_call(
        functools.partial(contact_kernel, fields, part),
        in_specs=[VM] * len(args),
        out_specs=[VM] * len(fields),
        out_shape=[jax.ShapeDtypeStruct((384, N), F32)] * len(fields),
        compiler_params=limits(32),
        cost_estimate=pl.CostEstimate(
            flops=10**9 * len(fields), bytes_accessed=2 * 10**6, transcendentals=0
        ),
        name=name,
    )(*args)


def place_kernel(mine, recv, *refs):
    h = lax.axis_index("harm")
    out = refs[-1]
    for side in range(2):

        @pl.when(h == side)
        def _():
            for source, base in ((mine, 4 * side), (recv, 4 * (1 - side))):
                for ch in range(3):
                    for i in range(4):
                        rows = pl.ds(ch * 256 + base + i, 32, stride=8)
                        block = source[pl.ds((ch * 4 + i) * 32, 32), :]
                        if len(refs) == 2:
                            block = block - refs[0][rows, :]
                        out[rows, :] = block


def place(name, *args):
    return pl.pallas_call(
        place_kernel,
        in_specs=[VM] * len(args),
        out_specs=VM,
        out_shape=jax.ShapeDtypeStruct((768, N), F32),
        compiler_params=limits(8),
        cost_estimate=pl.CostEstimate(flops=10**6, bytes_accessed=2 * 10**6, transcendentals=0),
        name=name,
    )(*args)


def swap(x):
    return lax.ppermute(x, "harm", [(0, 1), (1, 0)])


def body(
    disp, direction, stick_state, contact_params, mistuning, group_ids,
    diag_stiff, cross_stiff, excitation,
):
    to_time, to_coef, diff, pair, hart = tables()
    packed, wide = pack(
        disp, direction, stick_state, contact_params, diag_stiff, cross_stiff,
        mistuning.reshape(1, N), group_ids.reshape(1, N), jnp.asarray(pair), jnp.asarray(hart),
    )
    got = lax.all_to_all(
        packed.reshape(256, 1, ROWS * N), ("sector", "harm"), 0, 0, tiled=True
    ).reshape(256 * ROWS, N)
    args = (wide, to_time, to_coef, diff)
    (send0,) = contact("send0", (0,), 1, got, *args)
    send0, got = lax.optimization_barrier((send0, got))
    recv0 = swap(send0)
    (send1,) = contact("send1", (1,), 1, got, *args)
    send1, got = lax.optimization_barrier((send1, got))
    recv1 = swap(send1)
    mine0, mine1 = contact("keep", (0, 1), 0, got, *args)
    shape = excitation.shape
    residual = place("place0", mine0, recv0, excitation.reshape(768, N))
    mine1, residual = lax.optimization_barrier((mine1, residual))
    jvp = place("place1", mine1, recv1)
    return residual.reshape(shape), jvp.reshape(shape)


def solution(mesh):
    in_specs = (
        P("sector", None, "harm", None),
        P("sector", None, "harm", None),
        P("sector", None, None),
        P("sector", None, None),
        P(),
        P(),
        P("harm", None),
        P("harm", None),
        P(None, "harm", "sector", None),
    )
    out_specs = (P(None, "harm", "sector", None), P(None, "harm", "sector", None))
    return jax.shard_map(body, mesh=mesh, in_specs=in_specs, out_specs=out_specs, check_vma=False)
```

```python
import functools
import math

import jax
import jax.numpy as jnp
import ml_dtypes
import numpy as np
from jax import lax
from jax.experimental import pallas as pl
from jax.experimental.pallas import tpu as pltpu
from jax.sharding import PartitionSpec as P

F32 = jnp.float32
BF16 = jnp.bfloat16
N = 128
HALF = 32
ROWS = 9


def split_np(table):
    hi = table.astype(ml_dtypes.bfloat16)
    lo = (table - hi.astype(np.float64)).astype(ml_dtypes.bfloat16)
    return hi, lo


def tables():
    t = np.arange(N)
    j = np.arange(64) // 2 + 1
    angle = 2 * np.pi * (j[:, None] * t[None, :] % N) / N
    basis = np.where(np.arange(64)[:, None] % 2 == 0, np.cos(angle), np.sin(angle))
    angle = 2 * np.pi * (t[:, None] * t[None, :] % N) / N
    hart = (np.cos(angle) + np.sin(angle)) / math.sqrt(N)
    hart_mirror = (np.cos(angle) - np.sin(angle)) / math.sqrt(N)
    hart_diff = hart - np.roll(hart, -1, axis=0)
    to_time, to_coef = [], []
    for h in range(2):
        own = np.roll(np.roll(basis, -32 * h, axis=0), -64 * h, axis=1)
        hi, lo = split_np(own.T)
        to_time.append(np.concatenate([hi, hi, lo], 1))
        hi, lo = split_np(own * (2.0 / N))
        to_coef.append(np.concatenate([hi, hi, lo], 1))
    hi, lo = split_np(hart_diff)
    diff = np.concatenate([hi, hi, lo], 0)
    hi, lo = split_np(np.concatenate([hart, hart_mirror], 1))
    pair = np.concatenate([hi, hi, lo], 0)
    return np.stack(to_time), np.stack(to_coef), diff, pair, hart.astype(np.float32)


def halves(x):
    hi = x.astype(BF16)
    lo = (x - hi.astype(F32)).astype(BF16)
    return hi, lo


def mm(a, b):
    return jnp.dot(a, b, preferred_element_type=F32)


def split_rows(x):
    hi, lo = halves(x)
    return jnp.concatenate([hi, lo, hi], 0)


def split_lanes(x):
    hi, lo = halves(x)
    return jnp.concatenate([hi, lo, hi], 1)


VM = pl.BlockSpec(memory_space=pltpu.VMEM)


def limits(megabytes):
    return pltpu.CompilerParams(vmem_limit_bytes=megabytes << 20)


def pack_kernel(
    disp, direction, stick, *refs
):
    small_hbm, (packed, pull_hat, vd, ve, vz), refs = refs[:6], refs[6:11], refs[11:]
    small, (scr0, scr1, turned, sem, small_sem) = refs[:6], refs[6:]
    params, diag, cross, mist, groups, hart = small
    h = lax.axis_index("harm")
    samples = pl.ds(pl.multiple_of(h * 64, 64), 64)
    first = [
        pltpu.make_async_copy(small_hbm[k], small[k], small_sem.at[k]) for k in range(6)
    ]
    copies = []
    for ch in range(3):
        copies.append(pltpu.make_async_copy(disp.at[0, ch], vd.at[ch], sem.at[ch]))
        copies.append(pltpu.make_async_copy(direction.at[0, ch], ve.at[ch], sem.at[3 + ch]))
    copies.append(pltpu.make_async_copy(stick.at[0, samples], vz, sem.at[6]))
    for copy in first + copies:
        copy.start()
    for copy in first:
        copy.wait()
    here = jnp.broadcast_to(groups[...].astype(F32), (N, N))
    same = (here == here.T).astype(F32)
    members = jnp.sum(same, axis=0, keepdims=True)
    row = lax.broadcasted_iota(jnp.int32, (N, N), 0)
    lane = lax.broadcasted_iota(jnp.int32, (N, N), 1)
    pull = ((row == lane).astype(F32) - same / members) * mist[...]
    pulled = jnp.dot(
        pull, hart[...], preferred_element_type=F32, precision=lax.Precision.HIGHEST
    )
    hi, lo = halves(pulled)
    pull_hat[...] = jnp.concatenate([hi, hi, lo], 0)

    turned[...] = jnp.concatenate([diag[...], cross[...]] * 2, 0).T
    column = turned[pl.ds(lax.axis_index("sector"), 1), :]
    column = jnp.broadcast_to(pltpu.roll(column, 8, 1), (32, N))
    column = pltpu.roll(column, 0, 1, stride=4, stride_axis=0)
    spot = lax.broadcasted_iota(jnp.int32, (32, N), 0)
    quad = lax.broadcasted_iota(jnp.int32, (32, N), 1) // 4
    for copy in copies:
        copy.wait()
    for k in range(8):
        cols = pl.ds(k * N, N)
        d = vd[:, :, cols].reshape(96, N)
        e = ve[:, :, cols].reshape(96, N)
        z = vz[:, cols].astype(F32)
        scr0[k] = jnp.concatenate([d, e[:32]], 0).T
        scr1[k] = jnp.concatenate([e[32:], z], 0).T
        base = 32 * ROWS * k
        for i in range(4):
            to = pl.ds(base + 2 * i, 32, stride=ROWS)
            packed[to, :] = scr0[k, pl.ds(i, 32, stride=4), :]
            to = pl.ds(base + 2 * i + 1, 32, stride=ROWS)
            packed[to, :] = scr1[k, pl.ds(i, 32, stride=4), :]
        p = params[0, :, pl.ds(k * N, N)]
        near = jnp.where(h == 0, p[0:1], p[2:3])
        second = pltpu.roll(jnp.where(h == 0, p[1:2], p[3:4]), 4, 1)
        last = jnp.where(quad == (spot + 1) % 32, second, column)
        packed[pl.ds(base + 8, 32, stride=ROWS), :] = jnp.where(quad == spot, near, last)


def pack(*args):
    return pl.pallas_call(
        pack_kernel,
        in_specs=[pl.BlockSpec(memory_space=pl.ANY)] * len(args),
        out_specs=[VM, VM],
        out_shape=[
            jax.ShapeDtypeStruct((256 * ROWS, N), F32),
            jax.ShapeDtypeStruct((384, N), BF16),
        ],
        scratch_shapes=[
            pltpu.VMEM((3, 32, 8 * N), F32),
            pltpu.VMEM((3, 32, 8 * N), F32),
            pltpu.VMEM((64, 8 * N), jnp.int32),
        ]
        + [pltpu.VMEM(a.shape, a.dtype) for a in args[3:]]
        + [
            pltpu.VMEM((8, N, N), F32),
            pltpu.VMEM((8, N, N), F32),
            pltpu.VMEM((N, N), F32),
            pltpu.SemaphoreType.DMA((7,)),
            pltpu.SemaphoreType.DMA((6,)),
        ],
        compiler_params=limits(40),
        name="pack",
    )(*[pltpu.with_memory_space_constraint(a, pltpu.HBM) for a in args])


def contact_kernel(
    fields, part, got, pair, pull_hat, to_time, to_coef, diff, *outs
):
    h = lax.axis_index("harm")
    spot = (lax.axis_index("sector") * 2 + h) % 32
    step = 2 * ROWS
    tall, stiff = [], []
    for half in range(2):
        block = got[pl.ds(half * ROWS + 8, N, stride=step), :]
        block = pltpu.roll(block, (N - 4 * spot) % N, 1).T
        for at in range(2):
            tall.append(
                jnp.concatenate([block[4 * at + i : 4 * at + i + 1] for i in range(4)], 1)
            )
        stiff.append(block[8:72])
    stiff = jnp.where(h == part, stiff[0], stiff[1])
    diag, cross = stiff[0:HALF], stiff[HALF:64]
    n0, kn, kt, mu = tall
    states = [[[], [], []], [[], [], []]]
    stick = []
    for i in range(4):
        parts = []
        for half in (h, 1 - h):
            left = got[pl.ds(half * ROWS + 2 * i, N, stride=step), :].T
            right = got[pl.ds(half * ROWS + 2 * i + 1, N, stride=step), :].T
            parts.append((left, right))
        for q in range(3 + 3 * max(fields)):
            side, at = (0, q) if q < 4 else (1, q - 4)
            coefs = [p[side][HALF * at : HALF * at + HALF] for p in parts]
            states[q // 3][q % 3].append(coefs)
        stick.append(jnp.concatenate([p[1][64:128] for p in parts], 0))
    stick = jnp.concatenate(stick, 1)
    wave = to_time[h]

    def gap_of(state):
        all_coefs = [jnp.concatenate(c, 0) for ch in state for c in ch]
        rel = [f - pltpu.roll(f, N - 1, 1) for f in all_coefs]
        out = mm(wave, split_rows(jnp.concatenate(rel, 1)))
        return jnp.split(out, 3, axis=1)

    g0, g1, g2 = gap_of(states[0])
    touching = stick < 1.5
    sticking = stick < 0.5
    normal = n0 + kn * g0
    inv = lax.rsqrt(g1 * g1 + g2 * g2 + 1.0)
    zero = jnp.zeros_like(g0)
    gain = mu * normal * inv
    coef = jnp.where(sticking, kt, jnp.where(touching, gain, zero))
    for w, out in zip(fields, outs):
        if w == 0:
            traction = [jnp.where(touching, normal, zero), coef * g1, coef * g2]
        else:
            d0, d1, d2 = gap_of(states[1])
            dnormal = kn * d0
            proj = (g1 * d1 + g2 * d2) * (inv * inv)
            rate = mu * dnormal * inv - gain * proj
            rate = jnp.where(sticking, zero, jnp.where(touching, rate, zero))
            traction = [
                jnp.where(touching, dnormal, zero),
                coef * d1 + rate * g1,
                coef * d2 + rate * g2,
            ]
        weights = to_coef[h, HALF * part : HALF * part + HALF]
        load = mm(weights, split_rows(jnp.concatenate(traction, 1)))
        load = jnp.concatenate([load[:, N * q : N * q + N] for q in range(12)], 0)
        x = jnp.concatenate([c[part] for ch in states[w] for c in ch], 0)
        x = split_lanes(x)
        spec = mm(x, pair[...])
        total = mm(x, pull_hat[...]) + mm(split_lanes(load), diff[...])
        for q in range(12):
            rows = slice(HALF * q, HALF * q + HALF)
            out[rows, :] = (
                diag * spec[rows, 0:N] + cross * spec[rows, N : 2 * N] + total[rows]
            )


def contact(name, fields, part, *args):
    return pl.pallas_call(
        functools.partial(contact_kernel, fields, part),
        in_specs=[VM] * len(args),
        out_specs=[VM] * len(fields),
        out_shape=[jax.ShapeDtypeStruct((384, N), F32)] * len(fields),
        compiler_params=limits(32),
        cost_estimate=pl.CostEstimate(
            flops=10**9 * len(fields), bytes_accessed=2 * 10**6, transcendentals=0
        ),
        name=name,
    )(*args)


def place_kernel(mine, recv, *refs):
    h = lax.axis_index("harm")
    out = refs[-1]
    for side in range(2):

        @pl.when(h == side)
        def _():
            for source, base in ((mine, 4 * side), (recv, 4 * (1 - side))):
                for ch in range(3):
                    for i in range(4):
                        rows = pl.ds(ch * 256 + base + i, 32, stride=8)
                        block = source[pl.ds((ch * 4 + i) * 32, 32), :]
                        if len(refs) == 2:
                            block = block - refs[0][rows, :]
                        out[rows, :] = block


def place(name, *args):
    return pl.pallas_call(
        place_kernel,
        in_specs=[VM] * len(args),
        out_specs=VM,
        out_shape=jax.ShapeDtypeStruct((768, N), F32),
        compiler_params=limits(8),
        cost_estimate=pl.CostEstimate(flops=10**6, bytes_accessed=2 * 10**6, transcendentals=0),
        name=name,
    )(*args)


def swap(x):
    return lax.ppermute(x, "harm", [(0, 1), (1, 0)])


def body(
    disp, direction, stick_state, contact_params, mistuning, group_ids,
    diag_stiff, cross_stiff, excitation,
):
    to_time, to_coef, diff, pair, hart = tables()
    packed, pull_hat = pack(
        disp, direction, stick_state, contact_params, diag_stiff, cross_stiff,
        mistuning.reshape(1, N), group_ids.reshape(1, N), jnp.asarray(hart),
    )
    got = lax.all_to_all(
        packed.reshape(256, 1, ROWS * N), ("sector", "harm"), 0, 0, tiled=True
    ).reshape(256 * ROWS, N)
    args = (pair, pull_hat, to_time, to_coef, diff)
    (send0,) = contact("send0", (0,), 1, got, *args)
    send0, got = lax.optimization_barrier((send0, got))
    recv0 = swap(send0)
    (send1,) = contact("send1", (1,), 1, got, *args)
    send1, got = lax.optimization_barrier((send1, got))
    recv1 = swap(send1)
    mine0, mine1 = contact("keep", (0, 1), 0, got, *args)
    shape = excitation.shape
    residual = place("place0", mine0, recv0, excitation.reshape(768, N))
    mine1, residual = lax.optimization_barrier((mine1, residual))
    jvp = place("place1", mine1, recv1)
    return residual.reshape(shape), jvp.reshape(shape)


def solution(mesh):
    in_specs = (
        P("sector", None, "harm", None),
        P("sector", None, "harm", None),
        P("sector", None, None),
        P("sector", None, None),
        P(),
        P(),
        P("harm", None),
        P("harm", None),
        P(None, "harm", "sector", None),
    )
    out_specs = (P(None, "harm", "sector", None), P(None, "harm", "sector", None))
    return jax.shard_map(body, mesh=mesh, in_specs=in_specs, out_specs=out_specs, check_vma=False)
```

```python
import functools
import math

import jax
import jax.numpy as jnp
import ml_dtypes
import numpy as np
from jax import lax
from jax.experimental import pallas as pl
from jax.experimental.pallas import tpu as pltpu
from jax.sharding import PartitionSpec as P

F32 = jnp.float32
BF16 = jnp.bfloat16
N = 128
HALF = 32
ROWS = 9


def split_np(table):
    hi = table.astype(ml_dtypes.bfloat16)
    lo = (table - hi.astype(np.float64)).astype(ml_dtypes.bfloat16)
    return hi, lo


def tables():
    t = np.arange(N)
    j = np.arange(64) // 2 + 1
    angle = 2 * np.pi * (j[:, None] * t[None, :] % N) / N
    basis = np.where(np.arange(64)[:, None] % 2 == 0, np.cos(angle), np.sin(angle))
    angle = 2 * np.pi * (t[:, None] * t[None, :] % N) / N
    hart = (np.cos(angle) + np.sin(angle)) / math.sqrt(N)
    hart_mirror = (np.cos(angle) - np.sin(angle)) / math.sqrt(N)
    hart_diff = hart - np.roll(hart, -1, axis=0)
    to_time, to_coef = [], []
    for h in range(2):
        own = np.roll(np.roll(basis, -32 * h, axis=0), -64 * h, axis=1)
        hi, lo = split_np(own.T)
        to_time.append(np.concatenate([hi, hi, lo], 1))
        hi, lo = split_np(own * (2.0 / N))
        to_coef.append(np.concatenate([hi, hi, lo], 1))
    hi, lo = split_np(hart_diff)
    diff = np.concatenate([hi, hi, lo], 0)
    hi, lo = split_np(np.concatenate([hart, hart_mirror], 1))
    pair = np.concatenate([hi, hi, lo], 0)
    return np.stack(to_time), np.stack(to_coef), diff, pair, hart.astype(np.float32)


def halves(x):
    hi = x.astype(BF16)
    lo = (x - hi.astype(F32)).astype(BF16)
    return hi, lo


def mm(a, b):
    return jnp.dot(a, b, preferred_element_type=F32)


def split_rows(x):
    hi, lo = halves(x)
    return jnp.concatenate([hi, lo, hi], 0)


def split_lanes(x):
    hi, lo = halves(x)
    return jnp.concatenate([hi, lo, hi], 1)


VM = pl.BlockSpec(memory_space=pltpu.VMEM)


def limits(megabytes):
    return pltpu.CompilerParams(vmem_limit_bytes=megabytes << 20)


def pack_kernel(
    disp, direction, stick, *refs
):
    small_hbm, (packed, pull_hat, vd, ve, vz), refs = refs[:6], refs[6:11], refs[11:]
    small, (scr0, scr1, turned, sem, small_sem) = refs[:6], refs[6:]
    params, diag, cross, mist, groups, hart = small
    h = lax.axis_index("harm")
    samples = pl.ds(pl.multiple_of(h * 64, 64), 64)
    first = [
        pltpu.make_async_copy(small_hbm[k], small[k], small_sem.at[k]) for k in range(6)
    ]
    copies = []
    for ch in range(3):
        copies.append(pltpu.make_async_copy(disp.at[0, ch], vd.at[ch], sem.at[ch]))
        copies.append(pltpu.make_async_copy(direction.at[0, ch], ve.at[ch], sem.at[3 + ch]))
    copies.append(pltpu.make_async_copy(stick.at[0, samples], vz, sem.at[6]))
    for copy in first + copies:
        copy.start()
    for copy in first:
        copy.wait()
    here = jnp.broadcast_to(groups[...].astype(F32), (N, N))
    same = (here == here.T).astype(F32)
    members = jnp.sum(same, axis=0, keepdims=True)
    row = lax.broadcasted_iota(jnp.int32, (N, N), 0)
    lane = lax.broadcasted_iota(jnp.int32, (N, N), 1)
    pull = ((row == lane).astype(F32) - same / members) * mist[...]
    pulled = jnp.dot(
        pull, hart[...], preferred_element_type=F32, precision=lax.Precision.HIGHEST
    )
    hi, lo = halves(pulled)
    pull_hat[...] = jnp.concatenate([hi, hi, lo], 0)

    turned[...] = jnp.concatenate([diag[...], cross[...]] * 2, 0).T
    column = turned[pl.ds(lax.axis_index("sector"), 1), :]
    column = jnp.broadcast_to(pltpu.roll(column, 8, 1), (32, N))
    column = pltpu.roll(column, 0, 1, stride=4, stride_axis=0)
    spot = lax.broadcasted_iota(jnp.int32, (32, N), 0)
    quad = lax.broadcasted_iota(jnp.int32, (32, N), 1) // 4
    for copy in copies:
        copy.wait()
    for k in range(8):
        cols = pl.ds(k * N, N)
        d = vd[:, :, cols].reshape(96, N)
        e = ve[:, :, cols].reshape(96, N)
        z = vz[:, cols].astype(F32)
        scr0[k] = jnp.concatenate([d, e[:32]], 0).T
        scr1[k] = jnp.concatenate([e[32:], z], 0).T
        base = 32 * ROWS * k
        for i in range(4):
            to = pl.ds(base + 2 * i, 32, stride=ROWS)
            packed[to, :] = scr0[k, pl.ds(i, 32, stride=4), :]
            to = pl.ds(base + 2 * i + 1, 32, stride=ROWS)
            packed[to, :] = scr1[k, pl.ds(i, 32, stride=4), :]
        p = params[0, :, pl.ds(k * N, N)]
        near = jnp.where(h == 0, p[0:1], p[2:3])
        second = pltpu.roll(jnp.where(h == 0, p[1:2], p[3:4]), 4, 1)
        last = jnp.where(quad == (spot + 1) % 32, second, column)
        packed[pl.ds(base + 8, 32, stride=ROWS), :] = jnp.where(quad == spot, near, last)


def pack(*args):
    return pl.pallas_call(
        pack_kernel,
        in_specs=[pl.BlockSpec(memory_space=pl.ANY)] * len(args),
        out_specs=[VM, VM],
        out_shape=[
            jax.ShapeDtypeStruct((256 * ROWS, N), F32),
            jax.ShapeDtypeStruct((384, N), BF16),
        ],
        scratch_shapes=[
            pltpu.VMEM((3, 32, 8 * N), F32),
            pltpu.VMEM((3, 32, 8 * N), F32),
            pltpu.VMEM((64, 8 * N), jnp.int32),
        ]
        + [pltpu.VMEM(a.shape, a.dtype) for a in args[3:]]
        + [
            pltpu.VMEM((8, N, N), F32),
            pltpu.VMEM((8, N, N), F32),
            pltpu.VMEM((N, N), F32),
            pltpu.SemaphoreType.DMA((7,)),
            pltpu.SemaphoreType.DMA((6,)),
        ],
        compiler_params=limits(40),
        name="pack",
    )(*[pltpu.with_memory_space_constraint(a, pltpu.HBM) for a in args])


def contact_kernel(
    fields, part, got, pair, pull_hat, to_time, to_coef, diff, *outs
):
    h = lax.axis_index("harm")
    spot = (lax.axis_index("sector") * 2 + h) % 32
    step = 2 * ROWS
    tall, stiff = [], []
    for half in range(2):
        block = got[pl.ds(half * ROWS + 8, N, stride=step), :]
        block = pltpu.roll(block, (N - 4 * spot) % N, 1).T
        for at in range(2):
            tall.append(
                jnp.concatenate([block[4 * at + i : 4 * at + i + 1] for i in range(4)], 1)
            )
        stiff.append(block[8:72])
    stiff = jnp.where(h == part, stiff[0], stiff[1])
    diag, cross = stiff[0:HALF], stiff[HALF:64]
    n0, kn, kt, mu = tall
    states = [[[], [], []], [[], [], []]]
    stick = []
    for i in range(4):
        parts = []
        for half in (h, 1 - h):
            left = got[pl.ds(half * ROWS + 2 * i, N, stride=step), :].T
            right = got[pl.ds(half * ROWS + 2 * i + 1, N, stride=step), :].T
            parts.append((left, right))
        for q in range(3 + 3 * max(fields)):
            side, at = (0, q) if q < 4 else (1, q - 4)
            coefs = [p[side][HALF * at : HALF * at + HALF] for p in parts]
            states[q // 3][q % 3].append(coefs)
        stick.append(jnp.concatenate([p[1][64:128] for p in parts], 0))
    stick = jnp.concatenate(stick, 1)
    wave = to_time[h]

    def gap_of(state):
        all_coefs = [jnp.concatenate(c, 0) for ch in state for c in ch]
        rel = [f - pltpu.roll(f, N - 1, 1) for f in all_coefs]
        out = mm(wave, split_rows(jnp.concatenate(rel, 1)))
        return jnp.split(out, 3, axis=1)

    g0, g1, g2 = gap_of(states[0])
    touching = stick < 1.5
    sticking = stick < 0.5
    normal = n0 + kn * g0
    inv = lax.rsqrt(g1 * g1 + g2 * g2 + 1.0)
    zero = jnp.zeros_like(g0)
    gain = mu * normal * inv
    coef = jnp.where(sticking, kt, jnp.where(touching, gain, zero))
    for w, out in zip(fields, outs):
        if w == 0:
            traction = [jnp.where(touching, normal, zero), coef * g1, coef * g2]
        else:
            d0, d1, d2 = gap_of(states[1])
            dnormal = kn * d0
            proj = (g1 * d1 + g2 * d2) * (inv * inv)
            rate = mu * dnormal * inv - gain * proj
            rate = jnp.where(sticking, zero, jnp.where(touching, rate, zero))
            traction = [
                jnp.where(touching, dnormal, zero),
                coef * d1 + rate * g1,
                coef * d2 + rate * g2,
            ]
        weights = to_coef[h, HALF * part : HALF * part + HALF]
        load = mm(weights, split_rows(jnp.concatenate(traction, 1)))
        load = jnp.concatenate([load[:, N * q : N * q + N] for q in range(12)], 0)
        x = jnp.concatenate([c[part] for ch in states[w] for c in ch], 0)
        x = split_lanes(x)
        spec = mm(x, pair[...])
        total = mm(x, pull_hat[...]) + mm(split_lanes(load), diff[...])
        for q in range(12):
            rows = slice(HALF * q, HALF * q + HALF)
            out[rows, :] = (
                diag * spec[rows, 0:N] + cross * spec[rows, N : 2 * N] + total[rows]
            )


def contact(name, fields, part, *args):
    return pl.pallas_call(
        functools.partial(contact_kernel, fields, part),
        in_specs=[VM] * len(args),
        out_specs=[VM] * len(fields),
        out_shape=[jax.ShapeDtypeStruct((384, N), F32)] * len(fields),
        compiler_params=limits(32),
        cost_estimate=pl.CostEstimate(
            flops=10**9 * len(fields), bytes_accessed=2 * 10**6, transcendentals=0
        ),
        name=name,
    )(*args)


def place_kernel(mine, recv, *refs):
    h = lax.axis_index("harm")
    out, whole, sem = refs[-3:]
    leave = []
    for ch in range(3):
        for side in range(2):

            @pl.when(h == side)
            def _():
                for source, base in ((mine, 4 * side), (recv, 4 * (1 - side))):
                    for i in range(4):
                        rows = pl.ds(ch * 256 + base + i, 32, stride=8)
                        block = source[pl.ds((ch * 4 + i) * 32, 32), :]
                        if len(refs) == 4:
                            block = block - refs[0][rows, :]
                        whole[rows, :] = block

        span = pl.ds(ch * 256, 256)
        leave.append(pltpu.make_async_copy(whole.at[span], out.at[span], sem.at[ch]))
        leave[-1].start()
    for copy in leave:
        copy.wait()


def place(name, *args):
    return pl.pallas_call(
        place_kernel,
        in_specs=[VM] * len(args),
        out_specs=pl.BlockSpec(memory_space=pltpu.HBM),
        out_shape=jax.ShapeDtypeStruct((768, N), F32),
        scratch_shapes=[pltpu.VMEM((768, N), F32), pltpu.SemaphoreType.DMA((3,))],
        compiler_params=limits(8),
        cost_estimate=pl.CostEstimate(flops=10**6, bytes_accessed=2 * 10**6, transcendentals=0),
        name=name,
    )(*args)


def swap(x):
    return lax.ppermute(x, "harm", [(0, 1), (1, 0)])


def body(
    disp, direction, stick_state, contact_params, mistuning, group_ids,
    diag_stiff, cross_stiff, excitation,
):
    to_time, to_coef, diff, pair, hart = tables()
    packed, pull_hat = pack(
        disp, direction, stick_state, contact_params, diag_stiff, cross_stiff,
        mistuning.reshape(1, N), group_ids.reshape(1, N), jnp.asarray(hart),
    )
    got = lax.all_to_all(
        packed.reshape(256, 1, ROWS * N), ("sector", "harm"), 0, 0, tiled=True
    ).reshape(256 * ROWS, N)
    args = (pair, pull_hat, to_time, to_coef, diff)
    (send0,) = contact("send0", (0,), 1, got, *args)
    send0, got = lax.optimization_barrier((send0, got))
    recv0 = swap(send0)
    (send1,) = contact("send1", (1,), 1, got, *args)
    send1, got = lax.optimization_barrier((send1, got))
    recv1 = swap(send1)
    mine0, mine1 = contact("keep", (0, 1), 0, got, *args)
    shape = excitation.shape
    residual = place("place0", mine0, recv0, excitation.reshape(768, N))
    mine1, residual = lax.optimization_barrier((mine1, residual))
    jvp = place("place1", mine1, recv1)
    return residual.reshape(shape), jvp.reshape(shape)


def solution(mesh):
    in_specs = (
        P("sector", None, "harm", None),
        P("sector", None, "harm", None),
        P("sector", None, None),
        P("sector", None, None),
        P(),
        P(),
        P("harm", None),
        P("harm", None),
        P(None, "harm", "sector", None),
    )
    out_specs = (P(None, "harm", "sector", None), P(None, "harm", "sector", None))
    return jax.shard_map(body, mesh=mesh, in_specs=in_specs, out_specs=out_specs, check_vma=False)
```

```python
import functools
import math

import jax
import jax.numpy as jnp
import ml_dtypes
import numpy as np
from jax import lax
from jax.experimental import pallas as pl
from jax.experimental.pallas import tpu as pltpu
from jax.sharding import PartitionSpec as P

F32 = jnp.float32
BF16 = jnp.bfloat16
N = 128
HALF = 32
ROWS = 9


def split_np(table):
    hi = table.astype(ml_dtypes.bfloat16)
    lo = (table - hi.astype(np.float64)).astype(ml_dtypes.bfloat16)
    return hi, lo


def tables():
    t = np.arange(N)
    j = np.arange(64) // 2 + 1
    angle = 2 * np.pi * (j[:, None] * t[None, :] % N) / N
    basis = np.where(np.arange(64)[:, None] % 2 == 0, np.cos(angle), np.sin(angle))
    angle = 2 * np.pi * (t[:, None] * t[None, :] % N) / N
    hart = (np.cos(angle) + np.sin(angle)) / math.sqrt(N)
    hart_mirror = (np.cos(angle) - np.sin(angle)) / math.sqrt(N)
    hart_diff = hart - np.roll(hart, -1, axis=0)
    to_time, to_coef = [], []
    for h in range(2):
        own = np.roll(basis, -32 * h, axis=0)
        hi, lo = split_np(own.T)
        to_time.append(np.concatenate([hi, hi, lo], 1))
        hi, lo = split_np(own * (2.0 / N))
        to_coef.append(np.concatenate([hi, hi, lo], 1))
    hi, lo = split_np(hart_diff)
    diff = np.concatenate([hi, hi, lo], 0)
    hi, lo = split_np(np.concatenate([hart, hart_mirror], 1))
    pair = np.concatenate([hi, hi, lo], 0)
    return np.stack(to_time), np.stack(to_coef), diff, pair, hart.astype(np.float32)


def halves(x):
    hi = x.astype(BF16)
    lo = (x - hi.astype(F32)).astype(BF16)
    return hi, lo


def mm(a, b):
    return jnp.dot(a, b, preferred_element_type=F32)


def split_rows(x):
    hi, lo = halves(x)
    return jnp.concatenate([hi, lo, hi], 0)


def split_lanes(x):
    hi, lo = halves(x)
    return jnp.concatenate([hi, lo, hi], 1)


VM = pl.BlockSpec(memory_space=pltpu.VMEM)


def limits(megabytes):
    return pltpu.CompilerParams(vmem_limit_bytes=megabytes << 20)


def pack_kernel(
    disp, direction, stick, *refs
):
    small_hbm, (packed, pull_hat, vd, ve, vz), refs = refs[:6], refs[6:11], refs[11:]
    small, (scr0, scr1, turned, sem, small_sem) = refs[:6], refs[6:]
    params, diag, cross, mist, groups, hart = small
    h = lax.axis_index("harm")
    samples = pl.ds(pl.multiple_of(h * 64, 64), 64)
    first = [
        pltpu.make_async_copy(small_hbm[k], small[k], small_sem.at[k]) for k in range(6)
    ]
    copies = []
    for ch in range(3):
        copies.append(pltpu.make_async_copy(disp.at[0, ch], vd.at[ch], sem.at[ch]))
        copies.append(pltpu.make_async_copy(direction.at[0, ch], ve.at[ch], sem.at[3 + ch]))
    copies.append(pltpu.make_async_copy(stick.at[0, samples], vz, sem.at[6]))
    for copy in first + copies:
        copy.start()
    for copy in first:
        copy.wait()
    here = jnp.broadcast_to(groups[...].astype(F32), (N, N))
    same = (here == here.T).astype(F32)
    members = jnp.sum(same, axis=0, keepdims=True)
    row = lax.broadcasted_iota(jnp.int32, (N, N), 0)
    lane = lax.broadcasted_iota(jnp.int32, (N, N), 1)
    pull = ((row == lane).astype(F32) - same / members) * mist[...]
    pulled = jnp.dot(
        pull, hart[...], preferred_element_type=F32, precision=lax.Precision.HIGHEST
    )
    hi, lo = halves(pulled)
    pull_hat[...] = jnp.concatenate([hi, hi, lo], 0)

    turned[...] = jnp.concatenate([diag[...], cross[...]] * 2, 0).T
    column = turned[pl.ds(lax.axis_index("sector"), 1), :]
    column = jnp.broadcast_to(pltpu.roll(column, 8, 1), (32, N))
    column = pltpu.roll(column, 0, 1, stride=4, stride_axis=0)
    spot = lax.broadcasted_iota(jnp.int32, (32, N), 0)
    quad = lax.broadcasted_iota(jnp.int32, (32, N), 1) // 4
    for copy in copies:
        copy.wait()
    for k in range(8):
        cols = pl.ds(k * N, N)
        d = vd[:, :, cols].reshape(96, N)
        e = ve[:, :, cols].reshape(96, N)
        z = vz[:, cols].astype(F32)
        scr0[k] = jnp.concatenate([d, e[:32]], 0).T
        mixed = jnp.where(
            h == 0, jnp.concatenate([z, e[32:]], 0), jnp.concatenate([e[32:], z], 0)
        )
        scr1[k] = mixed.T
        base = 32 * ROWS * k
        for i in range(4):
            to = pl.ds(base + 2 * i, 32, stride=ROWS)
            packed[to, :] = scr0[k, pl.ds(i, 32, stride=4), :]
            to = pl.ds(base + 2 * i + 1, 32, stride=ROWS)
            packed[to, :] = scr1[k, pl.ds(i, 32, stride=4), :]
        p = params[0, :, pl.ds(k * N, N)]
        near = jnp.where(h == 0, p[0:1], p[2:3])
        second = pltpu.roll(jnp.where(h == 0, p[1:2], p[3:4]), 4, 1)
        last = jnp.where(quad == (spot + 1) % 32, second, column)
        packed[pl.ds(base + 8, 32, stride=ROWS), :] = jnp.where(quad == spot, near, last)


def pack(*args):
    return pl.pallas_call(
        pack_kernel,
        in_specs=[pl.BlockSpec(memory_space=pl.ANY)] * len(args),
        out_specs=[VM, VM],
        out_shape=[
            jax.ShapeDtypeStruct((256 * ROWS, N), F32),
            jax.ShapeDtypeStruct((384, N), BF16),
        ],
        scratch_shapes=[
            pltpu.VMEM((3, 32, 8 * N), F32),
            pltpu.VMEM((3, 32, 8 * N), F32),
            pltpu.VMEM((64, 8 * N), jnp.int32),
        ]
        + [pltpu.VMEM(a.shape, a.dtype) for a in args[3:]]
        + [
            pltpu.VMEM((8, N, N), F32),
            pltpu.VMEM((8, N, N), F32),
            pltpu.VMEM((N, N), F32),
            pltpu.SemaphoreType.DMA((7,)),
            pltpu.SemaphoreType.DMA((6,)),
        ],
        compiler_params=limits(40),
        name="pack",
    )(*[pltpu.with_memory_space_constraint(a, pltpu.HBM) for a in args])


def contact_kernel(
    fields, part, got, pair, pull_hat, to_time, to_coef, diff, *outs
):
    h = lax.axis_index("harm")
    spot = (lax.axis_index("sector") * 2 + h) % 32
    step = 2 * ROWS
    tall, stiff = [], []
    for half in range(2):
        block = got[pl.ds(half * ROWS + 8, N, stride=step), :]
        block = pltpu.roll(block, (N - 4 * spot) % N, 1).T
        for at in range(2):
            tall.append(
                jnp.concatenate([block[4 * at + i : 4 * at + i + 1] for i in range(4)], 1)
            )
        stiff.append(block[8:72])
    stiff = jnp.where(h == part, stiff[0], stiff[1])
    diag, cross = stiff[0:HALF], stiff[HALF:64]
    n0, kn, kt, mu = tall
    states = [[[], [], []], [[], [], []]]
    stick = []
    lane = lax.broadcasted_iota(jnp.int32, (N, N), 1)
    for i in range(4):
        lefts = [got[pl.ds(b * ROWS + 2 * i, N, stride=step), :].T for b in (h, 1 - h)]
        rights = [got[pl.ds(b * ROWS + 2 * i + 1, N, stride=step), :] for b in range(2)]
        stick.append(jnp.where(lane < 64, rights[0], rights[1]).T)
        for ch in range(3):
            states[0][ch].append([p[HALF * ch : HALF * ch + HALF] for p in lefts])
        if max(fields):
            states[1][0].append([p[96:128] for p in lefts])
            moved = jnp.where(lane < 64, rights[1], rights[0]).T
            low, high = moved[0:64], moved[64:128]
            both = [jnp.where(h == 0, high, low), jnp.where(h == 0, low, high)]
            for ch in (1, 2):
                rows = slice(HALF * (ch - 1), HALF * ch)
                states[1][ch].append([p[rows] for p in both])
    stick = jnp.concatenate(stick, 1)
    wave = to_time[h]

    def gap_of(state):
        all_coefs = [jnp.concatenate(c, 0) for ch in state for c in ch]
        rel = [f - pltpu.roll(f, N - 1, 1) for f in all_coefs]
        out = mm(wave, split_rows(jnp.concatenate(rel, 1)))
        return jnp.split(out, 3, axis=1)

    g0, g1, g2 = gap_of(states[0])
    touching = stick < 1.5
    sticking = stick < 0.5
    normal = n0 + kn * g0
    inv = lax.rsqrt(g1 * g1 + g2 * g2 + 1.0)
    zero = jnp.zeros_like(g0)
    gain = mu * normal * inv
    coef = jnp.where(sticking, kt, jnp.where(touching, gain, zero))
    for w, out in zip(fields, outs):
        if w == 0:
            traction = [jnp.where(touching, normal, zero), coef * g1, coef * g2]
        else:
            d0, d1, d2 = gap_of(states[1])
            dnormal = kn * d0
            proj = (g1 * d1 + g2 * d2) * (inv * inv)
            rate = mu * dnormal * inv - gain * proj
            rate = jnp.where(sticking, zero, jnp.where(touching, rate, zero))
            traction = [
                jnp.where(touching, dnormal, zero),
                coef * d1 + rate * g1,
                coef * d2 + rate * g2,
            ]
        weights = to_coef[h, HALF * part : HALF * part + HALF]
        load = mm(weights, split_rows(jnp.concatenate(traction, 1)))
        load = jnp.concatenate([load[:, N * q : N * q + N] for q in range(12)], 0)
        x = jnp.concatenate([c[part] for ch in states[w] for c in ch], 0)
        x = split_lanes(x)
        spec = mm(x, pair[...])
        total = mm(x, pull_hat[...]) + mm(split_lanes(load), diff[...])
        for q in range(12):
            rows = slice(HALF * q, HALF * q + HALF)
            out[rows, :] = (
                diag * spec[rows, 0:N] + cross * spec[rows, N : 2 * N] + total[rows]
            )


def contact(name, fields, part, *args):
    return pl.pallas_call(
        functools.partial(contact_kernel, fields, part),
        in_specs=[VM] * len(args),
        out_specs=[VM] * len(fields),
        out_shape=[jax.ShapeDtypeStruct((384, N), F32)] * len(fields),
        compiler_params=limits(32),
        cost_estimate=pl.CostEstimate(
            flops=10**9 * len(fields), bytes_accessed=2 * 10**6, transcendentals=0
        ),
        name=name,
    )(*args)


def place_kernel(mine, recv, *refs):
    h = lax.axis_index("harm")
    out, whole, sem = refs[-3:]
    leave = []
    for ch in range(3):
        for side in range(2):

            @pl.when(h == side)
            def _():
                for source, base in ((mine, 4 * side), (recv, 4 * (1 - side))):
                    for i in range(4):
                        rows = pl.ds(ch * 256 + base + i, 32, stride=8)
                        block = source[pl.ds((ch * 4 + i) * 32, 32), :]
                        if len(refs) == 4:
                            block = block - refs[0][rows, :]
                        whole[rows, :] = block

        span = pl.ds(ch * 256, 256)
        leave.append(pltpu.make_async_copy(whole.at[span], out.at[span], sem.at[ch]))
        leave[-1].start()
    for copy in leave:
        copy.wait()


def place(name, *args):
    return pl.pallas_call(
        place_kernel,
        in_specs=[VM] * len(args),
        out_specs=pl.BlockSpec(memory_space=pltpu.HBM),
        out_shape=jax.ShapeDtypeStruct((768, N), F32),
        scratch_shapes=[pltpu.VMEM((768, N), F32), pltpu.SemaphoreType.DMA((3,))],
        compiler_params=limits(8),
        cost_estimate=pl.CostEstimate(flops=10**6, bytes_accessed=2 * 10**6, transcendentals=0),
        name=name,
    )(*args)


def swap(x):
    return lax.ppermute(x, "harm", [(0, 1), (1, 0)])


def body(
    disp, direction, stick_state, contact_params, mistuning, group_ids,
    diag_stiff, cross_stiff, excitation,
):
    to_time, to_coef, diff, pair, hart = tables()
    packed, pull_hat = pack(
        disp, direction, stick_state, contact_params, diag_stiff, cross_stiff,
        mistuning.reshape(1, N), group_ids.reshape(1, N), jnp.asarray(hart),
    )
    got = lax.all_to_all(
        packed.reshape(256, 1, ROWS * N), ("sector", "harm"), 0, 0, tiled=True
    ).reshape(256 * ROWS, N)
    args = (pair, pull_hat, to_time, to_coef, diff)
    (send0,) = contact("send0", (0,), 1, got, *args)
    send0, got = lax.optimization_barrier((send0, got))
    recv0 = swap(send0)
    (send1,) = contact("send1", (1,), 1, got, *args)
    send1, got = lax.optimization_barrier((send1, got))
    recv1 = swap(send1)
    mine0, mine1 = contact("keep", (0, 1), 0, got, *args)
    shape = excitation.shape
    residual = place("place0", mine0, recv0, excitation.reshape(768, N))
    mine1, residual = lax.optimization_barrier((mine1, residual))
    jvp = place("place1", mine1, recv1)
    return residual.reshape(shape), jvp.reshape(shape)


def solution(mesh):
    in_specs = (
        P("sector", None, "harm", None),
        P("sector", None, "harm", None),
        P("sector", None, None),
        P("sector", None, None),
        P(),
        P(),
        P("harm", None),
        P("harm", None),
        P(None, "harm", "sector", None),
    )
    out_specs = (P(None, "harm", "sector", None), P(None, "harm", "sector", None))
    return jax.shard_map(body, mesh=mesh, in_specs=in_specs, out_specs=out_specs, check_vma=False)
```

```python
import functools
import math

import jax
import jax.numpy as jnp
import ml_dtypes
import numpy as np
from jax import lax
from jax.experimental import pallas as pl
from jax.experimental.pallas import tpu as pltpu
from jax.sharding import PartitionSpec as P

F32 = jnp.float32
BF16 = jnp.bfloat16
N = 128
HALF = 32
ROWS = 9


def split_np(table):
    hi = table.astype(ml_dtypes.bfloat16)
    lo = (table - hi.astype(np.float64)).astype(ml_dtypes.bfloat16)
    return hi, lo


def tables():
    t = np.arange(N)
    j = np.arange(64) // 2 + 1
    angle = 2 * np.pi * (j[:, None] * t[None, :] % N) / N
    basis = np.where(np.arange(64)[:, None] % 2 == 0, np.cos(angle), np.sin(angle))
    angle = 2 * np.pi * (t[:, None] * t[None, :] % N) / N
    hart = (np.cos(angle) + np.sin(angle)) / math.sqrt(N)
    hart_mirror = (np.cos(angle) - np.sin(angle)) / math.sqrt(N)
    hart_diff = hart - np.roll(hart, -1, axis=0)
    to_time, to_coef = [], []
    for h in range(2):
        own = np.roll(np.roll(basis, -32 * h, axis=0), -64 * h, axis=1)
        hi, lo = split_np(own.T)
        to_time.append(np.concatenate([hi, hi, lo], 1))
        hi, lo = split_np(own * (2.0 / N))
        to_coef.append(np.concatenate([hi, hi, lo], 1))
    hi, lo = split_np(hart_diff)
    diff = np.concatenate([hi, hi, lo], 0)
    hi, lo = split_np(np.concatenate([hart, hart_mirror], 1))
    pair = np.concatenate([hi, hi, lo], 0)
    return np.stack(to_time), np.stack(to_coef), diff, pair, hart.astype(np.float32)


def halves(x):
    hi = x.astype(BF16)
    lo = (x - hi.astype(F32)).astype(BF16)
    return hi, lo


def mm(a, b):
    return jnp.dot(a, b, preferred_element_type=F32)


def split_rows(x):
    hi, lo = halves(x)
    return jnp.concatenate([hi, lo, hi], 0)


def split_lanes(x):
    hi, lo = halves(x)
    return jnp.concatenate([hi, lo, hi], 1)


VM = pl.BlockSpec(memory_space=pltpu.VMEM)


def limits(megabytes):
    return pltpu.CompilerParams(vmem_limit_bytes=megabytes << 20)


def pack_kernel(
    disp, direction, stick, *refs
):
    small_hbm, (packed, pull_hat, vd, ve, vz), refs = refs[:6], refs[6:11], refs[11:]
    small, (scr0, scr1, turned, sem, small_sem) = refs[:6], refs[6:]
    params, diag, cross, mist, groups, hart = small
    h = lax.axis_index("harm")
    samples = pl.ds(pl.multiple_of(h * 64, 64), 64)
    first = [
        pltpu.make_async_copy(small_hbm[k], small[k], small_sem.at[k]) for k in range(6)
    ]
    copies = [pltpu.make_async_copy(stick.at[0, samples], vz, sem.at[6])]
    for ch in range(3):
        copies.append(pltpu.make_async_copy(disp.at[0, ch], vd.at[ch], sem.at[ch]))
        copies.append(pltpu.make_async_copy(direction.at[0, ch], ve.at[ch], sem.at[3 + ch]))
    for copy in first + copies:
        copy.start()
    for copy in first:
        copy.wait()
    here = jnp.broadcast_to(groups[...].astype(F32), (N, N))
    same = (here == here.T).astype(F32)
    members = jnp.sum(same, axis=0, keepdims=True)
    row = lax.broadcasted_iota(jnp.int32, (N, N), 0)
    lane = lax.broadcasted_iota(jnp.int32, (N, N), 1)
    pull = ((row == lane).astype(F32) - same / members) * mist[...]
    pulled = jnp.dot(
        pull, hart[...], preferred_element_type=F32, precision=lax.Precision.HIGHEST
    )
    hi, lo = halves(pulled)
    pull_hat[...] = jnp.concatenate([hi, hi, lo], 0)

    turned[...] = jnp.concatenate([diag[...], cross[...]] * 2, 0).T
    column = turned[pl.ds(lax.axis_index("sector"), 1), :]
    column = jnp.broadcast_to(pltpu.roll(column, 8, 1), (32, N))
    column = pltpu.roll(column, 0, 1, stride=4, stride_axis=0)
    spot = lax.broadcasted_iota(jnp.int32, (32, N), 0)
    quad = lax.broadcasted_iota(jnp.int32, (32, N), 1) // 4
    for copy in copies:
        copy.wait()
    for k in range(8):
        cols = pl.ds(k * N, N)
        d = vd[:, :, cols].reshape(96, N)
        e = ve[:, :, cols].reshape(96, N)
        z = vz[:, cols].astype(F32)
        scr0[k] = jnp.concatenate([d, e[:32]], 0).T
        scr1[k] = jnp.concatenate([e[32:], z], 0).T
        base = 32 * ROWS * k
        for i in range(4):
            to = pl.ds(base + 2 * i, 32, stride=ROWS)
            packed[to, :] = scr0[k, pl.ds(i, 32, stride=4), :]
            to = pl.ds(base + 2 * i + 1, 32, stride=ROWS)
            packed[to, :] = scr1[k, pl.ds(i, 32, stride=4), :]
        p = params[0, :, pl.ds(k * N, N)]
        near = jnp.where(h == 0, p[0:1], p[2:3])
        second = pltpu.roll(jnp.where(h == 0, p[1:2], p[3:4]), 4, 1)
        last = jnp.where(quad == (spot + 1) % 32, second, column)
        packed[pl.ds(base + 8, 32, stride=ROWS), :] = jnp.where(quad == spot, near, last)


def pack(*args):
    return pl.pallas_call(
        pack_kernel,
        in_specs=[pl.BlockSpec(memory_space=pl.ANY)] * len(args),
        out_specs=[VM, VM],
        out_shape=[
            jax.ShapeDtypeStruct((256 * ROWS, N), F32),
            jax.ShapeDtypeStruct((384, N), BF16),
        ],
        scratch_shapes=[
            pltpu.VMEM((3, 32, 8 * N), F32),
            pltpu.VMEM((3, 32, 8 * N), F32),
            pltpu.VMEM((64, 8 * N), jnp.int32),
        ]
        + [pltpu.VMEM(a.shape, a.dtype) for a in args[3:]]
        + [
            pltpu.VMEM((8, N, N), F32),
            pltpu.VMEM((8, N, N), F32),
            pltpu.VMEM((N, N), F32),
            pltpu.SemaphoreType.DMA((7,)),
            pltpu.SemaphoreType.DMA((6,)),
        ],
        compiler_params=limits(40),
        name="pack",
    )(*[pltpu.with_memory_space_constraint(a, pltpu.HBM) for a in args])


def contact_kernel(
    fields, part, got, pair, pull_hat, to_time, to_coef, diff, *outs
):
    h = lax.axis_index("harm")
    spot = (lax.axis_index("sector") * 2 + h) % 32
    step = 2 * ROWS
    tall, stiff = [], []
    for half in range(2):
        block = got[pl.ds(half * ROWS + 8, N, stride=step), :]
        block = pltpu.roll(block, (N - 4 * spot) % N, 1).T
        for at in range(2):
            tall.append(
                jnp.concatenate([block[4 * at + i : 4 * at + i + 1] for i in range(4)], 1)
            )
        stiff.append(block[8:72])
    stiff = jnp.where(h == part, stiff[0], stiff[1])
    diag, cross = stiff[0:HALF], stiff[HALF:64]
    n0, kn, kt, mu = tall
    states = [[[], [], []], [[], [], []]]
    stick = []
    for i in range(4):
        parts = []
        for half in (h, 1 - h):
            left = got[pl.ds(half * ROWS + 2 * i, N, stride=step), :].T
            right = got[pl.ds(half * ROWS + 2 * i + 1, N, stride=step), :].T
            parts.append((left, right))
        for q in range(3 + 3 * max(fields)):
            side, at = (0, q) if q < 4 else (1, q - 4)
            coefs = [p[side][HALF * at : HALF * at + HALF] for p in parts]
            states[q // 3][q % 3].append(coefs)
        stick.append(jnp.concatenate([p[1][64:128] for p in parts], 0))
    stick = jnp.concatenate(stick, 1)
    wave = to_time[h]

    def gap_of(state):
        all_coefs = [jnp.concatenate(c, 0) for ch in state for c in ch]
        rel = [f - pltpu.roll(f, N - 1, 1) for f in all_coefs]
        out = mm(wave, split_rows(jnp.concatenate(rel, 1)))
        return jnp.split(out, 3, axis=1)

    g0, g1, g2 = gap_of(states[0])
    touching = stick < 1.5
    sticking = stick < 0.5
    normal = n0 + kn * g0
    inv = lax.rsqrt(g1 * g1 + g2 * g2 + 1.0)
    zero = jnp.zeros_like(g0)
    gain = mu * normal * inv
    coef = jnp.where(sticking, kt, jnp.where(touching, gain, zero))
    for w, out in zip(fields, outs):
        if w == 0:
            traction = [jnp.where(touching, normal, zero), coef * g1, coef * g2]
        else:
            d0, d1, d2 = gap_of(states[1])
            dnormal = kn * d0
            proj = (g1 * d1 + g2 * d2) * (inv * inv)
            rate = mu * dnormal * inv - gain * proj
            rate = jnp.where(sticking, zero, jnp.where(touching, rate, zero))
            traction = [
                jnp.where(touching, dnormal, zero),
                coef * d1 + rate * g1,
                coef * d2 + rate * g2,
            ]
        weights = to_coef[h, HALF * part : HALF * part + HALF]
        load = mm(weights, split_rows(jnp.concatenate(traction, 1)))
        load = jnp.concatenate([load[:, N * q : N * q + N] for q in range(12)], 0)
        x = jnp.concatenate([c[part] for ch in states[w] for c in ch], 0)
        x = split_lanes(x)
        spec = mm(x, pair[...])
        total = mm(x, pull_hat[...]) + mm(split_lanes(load), diff[...])
        for q in range(12):
            rows = slice(HALF * q, HALF * q + HALF)
            out[rows, :] = (
                diag * spec[rows, 0:N] + cross * spec[rows, N : 2 * N] + total[rows]
            )


def contact(name, fields, part, *args):
    return pl.pallas_call(
        functools.partial(contact_kernel, fields, part),
        in_specs=[VM] * len(args),
        out_specs=[VM] * len(fields),
        out_shape=[jax.ShapeDtypeStruct((384, N), F32)] * len(fields),
        compiler_params=limits(32),
        cost_estimate=pl.CostEstimate(
            flops=10**9 * len(fields), bytes_accessed=2 * 10**6, transcendentals=0
        ),
        name=name,
    )(*args)


def place_kernel(mine, recv, *refs):
    h = lax.axis_index("harm")
    out, whole, sem = refs[-3:]
    leave = []
    for ch in range(3):
        for side in range(2):

            @pl.when(h == side)
            def _():
                for source, base in ((mine, 4 * side), (recv, 4 * (1 - side))):
                    for i in range(4):
                        rows = pl.ds(ch * 256 + base + i, 32, stride=8)
                        block = source[pl.ds((ch * 4 + i) * 32, 32), :]
                        if len(refs) == 4:
                            block = block - refs[0][rows, :]
                        whole[rows, :] = block

        span = pl.ds(ch * 256, 256)
        leave.append(pltpu.make_async_copy(whole.at[span], out.at[span], sem.at[ch]))
        leave[-1].start()
    for copy in leave:
        copy.wait()


def place(name, *args):
    return pl.pallas_call(
        place_kernel,
        in_specs=[VM] * len(args),
        out_specs=pl.BlockSpec(memory_space=pltpu.HBM),
        out_shape=jax.ShapeDtypeStruct((768, N), F32),
        scratch_shapes=[pltpu.VMEM((768, N), F32), pltpu.SemaphoreType.DMA((3,))],
        compiler_params=limits(8),
        cost_estimate=pl.CostEstimate(flops=10**6, bytes_accessed=2 * 10**6, transcendentals=0),
        name=name,
    )(*args)


def swap(x):
    return lax.ppermute(x, "harm", [(0, 1), (1, 0)])


def body(
    disp, direction, stick_state, contact_params, mistuning, group_ids,
    diag_stiff, cross_stiff, excitation,
):
    to_time, to_coef, diff, pair, hart = tables()
    packed, pull_hat = pack(
        disp, direction, stick_state, contact_params, diag_stiff, cross_stiff,
        mistuning.reshape(1, N), group_ids.reshape(1, N), jnp.asarray(hart),
    )
    got = lax.all_to_all(
        packed.reshape(256, 1, ROWS * N), ("sector", "harm"), 0, 0, tiled=True
    ).reshape(256 * ROWS, N)
    args = (pair, pull_hat, to_time, to_coef, diff)
    (send0,) = contact("send0", (0,), 1, got, *args)
    send0, got = lax.optimization_barrier((send0, got))
    recv0 = swap(send0)
    (send1,) = contact("send1", (1,), 1, got, *args)
    send1, got = lax.optimization_barrier((send1, got))
    recv1 = swap(send1)
    mine0, mine1 = contact("keep", (0, 1), 0, got, *args)
    shape = excitation.shape
    residual = place("place0", mine0, recv0, excitation.reshape(768, N))
    mine1, residual = lax.optimization_barrier((mine1, residual))
    jvp = place("place1", mine1, recv1)
    return residual.reshape(shape), jvp.reshape(shape)


def solution(mesh):
    in_specs = (
        P("sector", None, "harm", None),
        P("sector", None, "harm", None),
        P("sector", None, None),
        P("sector", None, None),
        P(),
        P(),
        P("harm", None),
        P("harm", None),
        P(None, "harm", "sector", None),
    )
    out_specs = (P(None, "harm", "sector", None), P(None, "harm", "sector", None))
    return jax.shard_map(body, mesh=mesh, in_specs=in_specs, out_specs=out_specs, check_vma=False)
```
